128 devices in a mesh: dp: 16 (over x, y), tensor: 8 (over z, core).
Axes of the slice: x: 4, y: 4, z: 4, core: 2. Of those that a mesh axis runs over, the one named last changes fastest.
Arguments:
- kv_part: bfloat16 [8, 4096, 12288], P('tensor', 'dp'), may hold values from -2 to 2
- queries: bfloat16 [8192, 6144], P('dp', 'tensor'), may hold values from -6 to 6
- w_out: bfloat16 [6144, 8192], P('tensor'), may hold values from -0.078125 to 0.078125
- d_out: bfloat16 [8192, 8192], P('dp', 'tensor'), may hold values from -48 to 48
- nbr_owner: int32 [128, 2], replicated, may hold values from 0 to 15, as said below
- nbr_slot: int32 [128, 2], replicated, may hold values from 0 to 1, as said below
Outputs:
- mixed: bfloat16 [8192, 8192], P('dp', 'tensor')
- d_kv: bfloat16 [4096, 12288], P('dp', 'tensor')
The draws below stay inside these ranges and needn't reach their ends.
Inputs may be any that keep to these rules, and one draw needn't show every extreme that they name: `nbr_owner`: the two neighbours of one span have different owners. `nbr_slot`: all neighbours that the spans of one dp index r (spans r * 8 to (r + 1) * 8 - 1) take from one owner have the same slot.
All inputs are finite; a program needn't handle non-finite values.
Results may differ from the reference program's by a relative error of at most 0.025.
Values may be sent and summed in bfloat16 or wider, within the bound.
A program may use at most 192 MiB of HBM per device.

```python
import jax
import jax.numpy as jnp
from jax import lax

D = 8192
HEADS = 48
HD = 128
SPAN = 64
NBR_LEN = 128
NB_DEV = 2
CH_DEV = 8
SPANS = 128
TOKENS = 8192
NBRS = 32
AW = 6144
KVW = 12288
N_DP = 16
N_TENSOR = 8


def neighbour_tables(key):
    base = jax.random.fold_in(key, 101)
    first_key, second_key, third_key, fourth_key = jax.random.split(base, 4)
    span_ids = jnp.arange(SPANS, dtype=jnp.int32)
    order = jax.random.permutation(first_key, N_DP).astype(jnp.int32)
    shifts = jax.random.randint(second_key, (SPANS,), 0, N_DP, dtype=jnp.int32)
    first = (order[span_ids % N_DP] + shifts[span_ids // N_DP]) % N_DP
    second = (first + jax.random.randint(third_key, (SPANS,), 1, N_DP, dtype=jnp.int32)) % N_DP
    owners = jnp.stack([first, second], axis=1)
    table = jax.random.randint(fourth_key, (N_DP, N_DP), 0, NB_DEV, dtype=jnp.int32)
    table = table.at[0, first[0]].set(NB_DEV - 1)
    table = table.at[0, second[0]].set(0)
    readers = span_ids // CH_DEV
    slots = table[readers[:, None], owners]
    return (owners, slots)


def draw_nbr_owner(key, part):
    return neighbour_tables(key)[0]


def draw_nbr_slot(key, part):
    return neighbour_tables(key)[1]


def draw_kv_part(key, part):
    spread = N_TENSOR ** (-0.5)
    shape = (N_TENSOR, NBRS * NBR_LEN, KVW)
    values = jnp.clip(jax.random.normal(jax.random.fold_in(key, 303), shape, jnp.float32) * spread, -2.0, 2.0)
    return values.astype(jnp.bfloat16)


def draw_queries(key, part):
    shape = (TOKENS, AW)
    values = jnp.clip(jax.random.normal(jax.random.fold_in(key, 404), shape, jnp.float32), -6.0, 6.0)
    return values.astype(jnp.bfloat16)


def block_scale(own_key, extent, cuts, least, top_value):
    gain, own = 1.0, jax.random.fold_in(own_key, 6)
    for dim, shards_of in cuts:
        draws = jnp.exp(jax.random.uniform(jax.random.fold_in(own, dim), (shards_of,), jnp.float32, least / len(cuts), top_value / len(cuts)))
        gain = gain * jnp.repeat(draws, extent[dim] // shards_of).reshape([-1 if axis == dim else 1 for axis in range(len(extent))])
    return gain


def scatter_about(rng, extent, deviation, limit, cuts=(), kind=jnp.bfloat16):
    result = deviation * jax.random.normal(rng, extent, jnp.float32)
    if cuts:
        result = result * block_scale(rng, extent, cuts, -0.22, 0.18)
    return jnp.clip(result, -limit, limit).astype(kind)


def setup_inputs(seed: int = 0) -> dict:
    seeds = jax.random.split(jax.random.key(seed), 7)
    return {
        "kv_part": draw_kv_part(jax.random.fold_in(seeds[6], 71), 0),
        "queries": draw_queries(jax.random.fold_in(seeds[6], 71), 0),
        "w_out": scatter_about(seeds[2], (AW, D), AW ** -0.5, 0.078125, ((0, 8),)),
        "d_out": scatter_about(seeds[3], (TOKENS, D), 8.0, 48.0, ((0, 16), (1, 8))),
        "nbr_owner": draw_nbr_owner(jax.random.fold_in(seeds[6], 71), 0),
        "nbr_slot": draw_nbr_slot(jax.random.fold_in(seeds[6], 71), 0),
    }


def reference(kv_part, queries, w_out, d_out, nbr_owner, nbr_slot):
    kv_sum = jnp.sum(kv_part.astype(jnp.float32), axis=0).astype(jnp.bfloat16)
    kv_blocks = kv_sum.reshape(NBRS, NBR_LEN * KVW)
    grad_attended = jnp.dot(d_out, w_out.T, preferred_element_type=jnp.float32).astype(jnp.bfloat16)
    factor = HD ** -0.5
    owner_ids = jnp.arange(N_DP, dtype=jnp.int32)
    neighbour_ids = jnp.arange(NBRS, dtype=jnp.int32)

    def per_reader(total, reader):
        owners = lax.dynamic_slice_in_dim(nbr_owner, reader * CH_DEV, CH_DEV, 0).reshape(2 * CH_DEV)
        slots = lax.dynamic_slice_in_dim(nbr_slot, reader * CH_DEV, CH_DEV, 0).reshape(2 * CH_DEV)
        picked = jnp.take(kv_blocks, owners * NB_DEV + slots, axis=0)
        layout = picked.reshape(CH_DEV, 2 * NBR_LEN, HEADS, 2, HD).astype(jnp.float32)
        keys = layout[:, :, :, 0]
        values = layout[:, :, :, 1]
        query_rows = lax.dynamic_slice_in_dim(queries, reader * CH_DEV * SPAN, CH_DEV * SPAN, 0)
        query_view = query_rows.astype(jnp.float32).reshape(CH_DEV, SPAN, HEADS, HD)
        scores = jnp.einsum("cqhd,ckhd->chqk", query_view, keys, precision=lax.Precision.HIGHEST) * factor
        top = jnp.max(scores, axis=-1, keepdims=True)
        expo = jnp.exp(scores - top)
        probs = expo / jnp.sum(expo, axis=-1, keepdims=True)
        probs_low = probs.astype(jnp.bfloat16).astype(jnp.float32)
        attended = jnp.einsum("chqk,ckhd->cqhd", probs_low, values, precision=lax.Precision.HIGHEST).astype(jnp.bfloat16)
        grad_rows = lax.dynamic_slice_in_dim(grad_attended, reader * CH_DEV * SPAN, CH_DEV * SPAN, 0)
        grad_view = grad_rows.astype(jnp.float32).reshape(CH_DEV, SPAN, HEADS, HD)
        grad_values = jnp.einsum("chqk,cqhd->ckhd", probs_low, grad_view, precision=lax.Precision.HIGHEST)
        grad_probs = jnp.einsum("cqhd,ckhd->chqk", grad_view, values, precision=lax.Precision.HIGHEST)
        grad_scores = probs * (grad_probs - jnp.sum(probs * grad_probs, axis=-1, keepdims=True))
        grad_scores = grad_scores.astype(jnp.bfloat16).astype(jnp.float32)
        grad_keys = jnp.einsum("chqk,cqhd->ckhd", grad_scores, query_view, precision=lax.Precision.HIGHEST) * factor
        grad_blocks = jnp.stack([grad_keys, grad_values], axis=3).reshape(2 * CH_DEV, NBR_LEN * KVW)
        read_table = (owners[:, None] == owner_ids[None, :]).astype(jnp.float32)
        per_owner = jnp.dot(read_table.T, grad_blocks, precision=lax.Precision.HIGHEST).astype(jnp.bfloat16)
        per_owner = lax.optimization_barrier(per_owner).astype(jnp.float32)
        hits = owners[:, None] == owner_ids[None, :]
        reads_from = jnp.any(hits, axis=0)
        slot_from = jnp.max(jnp.where(hits, slots[:, None], 0), axis=0)
        target = owner_ids * NB_DEV + slot_from
        routing = ((target[:, None] == neighbour_ids[None, :]) & reads_from[:, None]).astype(jnp.float32)
        total = total + jnp.dot(routing.T, per_owner, precision=lax.Precision.HIGHEST)
        return total, attended.reshape(CH_DEV * SPAN, AW)

    total, attended_all = lax.scan(per_reader, jnp.zeros((NBRS, NBR_LEN * KVW), jnp.float32), jnp.arange(N_DP, dtype=jnp.int32))
    attended_all = attended_all.reshape(TOKENS, AW)
    group_width = AW // N_TENSOR

    def add_group(group, running):
        columns = lax.dynamic_slice_in_dim(attended_all, group * group_width, group_width, 1)
        rows = lax.dynamic_slice_in_dim(w_out, group * group_width, group_width, 0)
        partial_value = jnp.dot(columns, rows, preferred_element_type=jnp.float32).astype(jnp.bfloat16)
        partial_value = lax.optimization_barrier(partial_value)
        return running + partial_value.astype(jnp.float32)

    mixed = lax.fori_loop(0, N_TENSOR, add_group, jnp.zeros((TOKENS, D), jnp.float32)).astype(jnp.bfloat16)
    d_kv = total.astype(jnp.bfloat16).reshape(NBRS * NBR_LEN, KVW)
    return mixed, d_kv
```

```python
import functools

import jax
import jax.numpy as jnp
from jax import lax
from jax.experimental import pallas as pl
from jax.experimental.pallas import tpu as pltpu
from jax.sharding import PartitionSpec as P

HD = 128
SPAN = 64
NBR_LEN = 128
NB_DEV = 2


def attention_kernel(heads, q_ref, kv_ref, g_ref, att_ref, dkv_ref):
    factor = HD ** (-0.5)
    for h in range(heads):
        cols = slice(h * HD, (h + 1) * HD)
        kcols = slice(2 * h * HD, 2 * h * HD + HD)
        vcols = slice(2 * h * HD + HD, 2 * (h + 1) * HD)
        q = q_ref[:, cols]
        g = g_ref[:, cols]
        k = jnp.concatenate([kv_ref[0, :, kcols], kv_ref[1, :, kcols]], axis=0)
        v = jnp.concatenate([kv_ref[0, :, vcols], kv_ref[1, :, vcols]], axis=0)
        scores = (
            lax.dot_general(q, k, (((1,), (1,)), ((), ())), preferred_element_type=jnp.float32)
            * factor
        )
        top = jnp.max(scores, axis=-1, keepdims=True)
        expo = jnp.exp(scores - top)
        probs = expo / jnp.sum(expo, axis=-1, keepdims=True)
        probs_low = probs.astype(jnp.bfloat16)
        attended = jnp.dot(probs_low, v, preferred_element_type=jnp.float32)
        att_ref[:, cols] = attended.astype(att_ref.dtype)
        grad_values = lax.dot_general(
            probs_low, g, (((0,), (0,)), ((), ())), preferred_element_type=jnp.float32
        )
        grad_probs = lax.dot_general(
            g, v, (((1,), (1,)), ((), ())), preferred_element_type=jnp.float32
        )
        grad_scores = probs * (grad_probs - jnp.sum(probs * grad_probs, axis=-1, keepdims=True))
        grad_scores = grad_scores.astype(jnp.bfloat16)
        grad_keys = (
            lax.dot_general(
                grad_scores, q, (((0,), (0,)), ((), ())), preferred_element_type=jnp.float32
            )
            * factor
        )
        dkv_ref[0, :, kcols] = grad_keys[:NBR_LEN]
        dkv_ref[1, :, kcols] = grad_keys[NBR_LEN:]
        dkv_ref[0, :, vcols] = grad_values[:NBR_LEN]
        dkv_ref[1, :, vcols] = grad_values[NBR_LEN:]


def attention(queries, neighbours, grad_attended):
    rows, width = queries.shape
    spans = rows // SPAN
    heads = width // HD
    kv_width = neighbours.shape[2]
    return pl.pallas_call(
        functools.partial(attention_kernel, heads),
        grid=(spans,),
        in_specs=[
            pl.BlockSpec((SPAN, width), lambda c: (c, 0)),
            pl.BlockSpec((2, NBR_LEN, kv_width), lambda c: (c, 0, 0)),
            pl.BlockSpec((SPAN, width), lambda c: (c, 0)),
        ],
        out_specs=[
            pl.BlockSpec((SPAN, width), lambda c: (c, 0)),
            pl.BlockSpec((2, NBR_LEN, kv_width), lambda c: (c, 0, 0)),
        ],
        out_shape=[
            jax.ShapeDtypeStruct((rows, width), jnp.bfloat16),
            jax.ShapeDtypeStruct(neighbours.shape, jnp.float32),
        ],
    )(queries, neighbours, grad_attended)


def local(kv_part, queries, w_out, d_out, nbr_owner, nbr_slot):
    dp_count = lax.axis_size("dp")
    reader = lax.axis_index("dp")
    head_width = w_out.shape[0]
    share_width = 2 * head_width
    span_count = queries.shape[0] // SPAN
    read_count = 2 * span_count
    block_width = NBR_LEN * share_width
    shares = lax.psum_scatter(kv_part[0], "tensor", scatter_dimension=1, tiled=True)
    share_blocks = shares.reshape(NB_DEV, NBR_LEN, share_width)
    owner_ids = jnp.arange(dp_count, dtype=jnp.int32)
    slot_ids = jnp.arange(NB_DEV, dtype=jnp.int32)
    owner_hits = nbr_owner[:, :, None] == owner_ids[None, None, :]
    per_reader = owner_hits.reshape(dp_count, read_count, dp_count)
    reads_from = jnp.any(per_reader, axis=1)
    slot_from = jnp.max(jnp.where(per_reader, nbr_slot.reshape(dp_count, read_count, 1), 0), axis=1)
    my_owner = lax.dynamic_slice_in_dim(nbr_owner, reader * span_count, span_count, 0).reshape(
        read_count
    )
    my_slot = lax.dynamic_slice_in_dim(nbr_slot, reader * span_count, span_count, 0).reshape(
        read_count
    )
    read_table = (my_owner[:, None] == owner_ids[None, :]).astype(jnp.float32)
    serving = lax.dynamic_index_in_dim(reads_from, reader, 1, False)
    serving_slot = lax.dynamic_index_in_dim(slot_from, reader, 1, False)
    owner_select = ((serving_slot[:, None] == slot_ids[None, :]) & serving[:, None]).astype(
        jnp.bfloat16
    )
    everyone = lax.all_gather(share_blocks, "dp", axis=0, tiled=True)
    neighbours = jnp.take(everyone, my_owner * NB_DEV + my_slot, axis=0)
    grad_attended = lax.dot_general(
        lax.all_gather(d_out, "tensor", axis=1, tiled=True),
        w_out,
        (((1,), (1,)), ((), ())),
        preferred_element_type=jnp.float32,
    ).astype(jnp.bfloat16)
    attended, grad_blocks = attention(queries, neighbours, grad_attended)
    partial_out = jnp.dot(attended, w_out, preferred_element_type=jnp.float32)
    mixed = lax.psum_scatter(
        partial_out.astype(jnp.bfloat16), "tensor", scatter_dimension=1, tiled=True
    )
    per_owner = lax.dot_general(
        read_table,
        grad_blocks.reshape(read_count, block_width),
        (((0,), (0,)), ((), ())),
        precision=lax.Precision.HIGHEST,
        preferred_element_type=jnp.float32,
    ).astype(jnp.bfloat16)
    returned = lax.all_to_all(per_owner, "dp", split_axis=0, concat_axis=0, tiled=True)
    owner_grad = lax.dot_general(
        owner_select, returned, (((0,), (0,)), ((), ())), preferred_element_type=jnp.float32
    )
    d_kv = owner_grad.astype(jnp.bfloat16).reshape(NB_DEV * NBR_LEN, share_width)
    return (mixed, d_kv)


def solution(mesh):
    placed = (
        P("tensor", "dp", None),
        P("dp", "tensor"),
        P("tensor", None),
        P("dp", "tensor"),
        P(),
        P(),
    )
    return jax.shard_map(
        local,
        mesh=mesh,
        in_specs=placed,
        out_specs=(P("dp", "tensor"), P("dp", "tensor")),
        check_vma=False,
    )
```

```python
import functools

import jax
import jax.numpy as jnp
from jax import lax
from jax.experimental import pallas as pl
from jax.experimental.pallas import tpu as pltpu
from jax.sharding import PartitionSpec as P

HD = 128
SPAN = 64
NBR_LEN = 128
NB_DEV = 2


def attention_kernel(heads, owner_ref, pick_ref, q_ref, first_ref, second_ref, g_ref, att_ref, out_ref, acc_ref):
    factor = HD ** (-0.5)
    span = pl.program_id(0)

    @pl.when(span == 0)
    def _():
        acc_ref[...] = jnp.zeros_like(acc_ref)

    first = owner_ref[2 * span]
    second = owner_ref[2 * span + 1]
    for h in range(heads):
        cols = slice(h * HD, (h + 1) * HD)
        kcols = slice(2 * h * HD, 2 * h * HD + HD)
        vcols = slice(2 * h * HD + HD, 2 * (h + 1) * HD)
        q = q_ref[:, cols]
        g = g_ref[:, cols]
        k = jnp.concatenate([first_ref[0, :, kcols], second_ref[0, :, kcols]], axis=0)
        v = jnp.concatenate([first_ref[0, :, vcols], second_ref[0, :, vcols]], axis=0)
        scores = (
            lax.dot_general(q, k, (((1,), (1,)), ((), ())), preferred_element_type=jnp.float32)
            * factor
        )
        top = jnp.max(scores, axis=-1, keepdims=True)
        expo = jnp.exp(scores - top)
        probs = expo / jnp.sum(expo, axis=-1, keepdims=True)
        probs_low = probs.astype(jnp.bfloat16)
        attended = jnp.dot(probs_low, v, preferred_element_type=jnp.float32)
        att_ref[:, cols] = attended.astype(att_ref.dtype)
        grad_values = lax.dot_general(
            probs_low, g, (((0,), (0,)), ((), ())), preferred_element_type=jnp.float32
        )
        grad_probs = lax.dot_general(
            g, v, (((1,), (1,)), ((), ())), preferred_element_type=jnp.float32
        )
        grad_scores = probs * (grad_probs - jnp.sum(probs * grad_probs, axis=-1, keepdims=True))
        grad_scores = grad_scores.astype(jnp.bfloat16)
        grad_keys = (
            lax.dot_general(
                grad_scores, q, (((0,), (0,)), ((), ())), preferred_element_type=jnp.float32
            )
            * factor
        )
        acc_ref[first, :, kcols] += grad_keys[:NBR_LEN]
        acc_ref[second, :, kcols] += grad_keys[NBR_LEN:]
        acc_ref[first, :, vcols] += grad_values[:NBR_LEN]
        acc_ref[second, :, vcols] += grad_values[NBR_LEN:]

    @pl.when(span == pl.num_programs(0) - 1)
    def _():
        out_ref[...] = acc_ref[...].astype(out_ref.dtype)


def attention(owners, picks, queries, everyone, grad_attended, owner_count):
    rows, width = queries.shape
    spans = rows // SPAN
    heads = width // HD
    kv_width = everyone.shape[2]
    grid_spec = pltpu.PrefetchScalarGridSpec(
        num_scalar_prefetch=2,
        grid=(spans,),
        in_specs=[
            pl.BlockSpec((SPAN, width), lambda c, o, n: (c, 0)),
            pl.BlockSpec((1, NBR_LEN, kv_width), lambda c, o, n: (n[2 * c], 0, 0)),
            pl.BlockSpec((1, NBR_LEN, kv_width), lambda c, o, n: (n[2 * c + 1], 0, 0)),
            pl.BlockSpec((SPAN, width), lambda c, o, n: (c, 0)),
        ],
        out_specs=[
            pl.BlockSpec((SPAN, width), lambda c, o, n: (c, 0)),
            pl.BlockSpec((owner_count, NBR_LEN, kv_width), lambda c, o, n: (0, 0, 0)),
        ],
        scratch_shapes=[pltpu.VMEM((owner_count, NBR_LEN, kv_width), jnp.float32)],
    )
    return pl.pallas_call(
        functools.partial(attention_kernel, heads),
        grid_spec=grid_spec,
        out_shape=[
            jax.ShapeDtypeStruct((rows, width), jnp.bfloat16),
            jax.ShapeDtypeStruct((owner_count, NBR_LEN, kv_width), jnp.bfloat16),
        ],
        compiler_params=pltpu.CompilerParams(
            dimension_semantics=("arbitrary",), vmem_limit_bytes=56 * 1024 * 1024
        ),
    )(owners, picks, queries, everyone, everyone, grad_attended)


def slot_sum_kernel(readers, select_ref, returned_ref, out_ref):
    for slot in range(NB_DEV):
        total = returned_ref[0].astype(jnp.float32) * select_ref[0, slot]
        for r in range(1, readers):
            total = total + returned_ref[r].astype(jnp.float32) * select_ref[r, slot]
        out_ref[slot] = total.astype(out_ref.dtype)


def slot_sum(select, returned):
    readers, length, width = returned.shape
    tile = 256
    return pl.pallas_call(
        functools.partial(slot_sum_kernel, readers),
        grid=(width // tile,),
        in_specs=[
            pl.BlockSpec(memory_space=pltpu.SMEM),
            pl.BlockSpec((readers, length, tile), lambda j: (0, 0, j)),
        ],
        out_specs=pl.BlockSpec((NB_DEV, length, tile), lambda j: (0, 0, j)),
        out_shape=jax.ShapeDtypeStruct((NB_DEV, length, width), jnp.bfloat16),
    )(select, returned)


def local(kv_part, queries, w_out, d_out, nbr_owner, nbr_slot):
    dp_count = lax.axis_size("dp")
    reader = lax.axis_index("dp")
    head_width = w_out.shape[0]
    share_width = 2 * head_width
    span_count = queries.shape[0] // SPAN
    read_count = 2 * span_count
    shares = lax.psum_scatter(kv_part[0], "tensor", scatter_dimension=1, tiled=True)
    share_blocks = shares.reshape(NB_DEV, NBR_LEN, share_width)
    owner_ids = jnp.arange(dp_count, dtype=jnp.int32)
    slot_ids = jnp.arange(NB_DEV, dtype=jnp.int32)
    owner_hits = nbr_owner[:, :, None] == owner_ids[None, None, :]
    per_reader = owner_hits.reshape(dp_count, read_count, dp_count)
    reads_from = jnp.any(per_reader, axis=1)
    slot_from = jnp.max(jnp.where(per_reader, nbr_slot.reshape(dp_count, read_count, 1), 0), axis=1)
    my_owner = lax.dynamic_slice_in_dim(nbr_owner, reader * span_count, span_count, 0).reshape(
        read_count
    )
    my_slot = lax.dynamic_slice_in_dim(nbr_slot, reader * span_count, span_count, 0).reshape(
        read_count
    )
    serving = lax.dynamic_index_in_dim(reads_from, reader, 1, False)
    serving_slot = lax.dynamic_index_in_dim(slot_from, reader, 1, False)
    owner_select = ((serving_slot[:, None] == slot_ids[None, :]) & serving[:, None]).astype(
        jnp.float32
    )
    everyone = lax.all_gather(share_blocks, "dp", axis=0, tiled=True)
    picks = my_owner * NB_DEV + my_slot
    tensor_count = lax.axis_size("tensor")
    spread = jnp.broadcast_to(d_out[None], (tensor_count,) + d_out.shape)
    gathered = lax.all_to_all(spread, "tensor", split_axis=0, concat_axis=0, tiled=True)
    grad_attended = jnp.einsum(
        "tqc,htc->qh",
        gathered,
        w_out.reshape(head_width, tensor_count, d_out.shape[1]),
        preferred_element_type=jnp.float32,
    ).astype(jnp.bfloat16)
    attended, per_owner = attention(my_owner, picks, queries, everyone, grad_attended, dp_count)
    partial_out = jnp.dot(attended, w_out, preferred_element_type=jnp.float32)
    mixed = lax.psum_scatter(
        partial_out.astype(jnp.bfloat16), "tensor", scatter_dimension=1, tiled=True
    )
    returned = lax.all_to_all(per_owner, "dp", split_axis=0, concat_axis=0, tiled=True)
    owner_grad = slot_sum(owner_select, returned)
    d_kv = owner_grad.reshape(NB_DEV * NBR_LEN, share_width)
    return (mixed, d_kv)


def solution(mesh):
    placed = (
        P("tensor", "dp", None),
        P("dp", "tensor"),
        P("tensor", None),
        P("dp", "tensor"),
        P(),
        P(),
    )
    return jax.shard_map(
        local,
        mesh=mesh,
        in_specs=placed,
        out_specs=(P("dp", "tensor"), P("dp", "tensor")),
        check_vma=False,
    )
```

```python
import functools

import jax
import jax.numpy as jnp
from jax import lax
from jax.experimental import pallas as pl
from jax.experimental.pallas import tpu as pltpu
from jax.sharding import PartitionSpec as P

HD = 128
SPAN = 64
NBR_LEN = 128
NB_DEV = 2


def attention_kernel(heads, owner_ref, pick_ref, q_ref, first_ref, second_ref, g_ref, att_ref, out_ref, acc_ref):
    factor = HD ** (-0.5)
    span = pl.program_id(0)

    @pl.when(span == 0)
    def _():
        acc_ref[...] = jnp.zeros_like(acc_ref)

    first = owner_ref[2 * span]
    second = owner_ref[2 * span + 1]
    for h in range(heads):
        cols = slice(h * HD, (h + 1) * HD)
        kcols = slice(2 * h * HD, 2 * h * HD + HD)
        vcols = slice(2 * h * HD + HD, 2 * (h + 1) * HD)
        q = q_ref[:, cols]
        g = g_ref[:, cols]
        k = jnp.concatenate([first_ref[0, :, kcols], second_ref[0, :, kcols]], axis=0)
        v = jnp.concatenate([first_ref[0, :, vcols], second_ref[0, :, vcols]], axis=0)
        scores = (
            lax.dot_general(q, k, (((1,), (1,)), ((), ())), preferred_element_type=jnp.float32)
            * factor
        )
        top = jnp.max(scores, axis=-1, keepdims=True)
        expo = jnp.exp(scores - top)
        probs = expo / jnp.sum(expo, axis=-1, keepdims=True)
        probs_low = probs.astype(jnp.bfloat16)
        attended = jnp.dot(probs_low, v, preferred_element_type=jnp.float32)
        att_ref[:, cols] = attended.astype(att_ref.dtype)
        grad_values = lax.dot_general(
            probs_low, g, (((0,), (0,)), ((), ())), preferred_element_type=jnp.float32
        )
        grad_probs = lax.dot_general(
            g, v, (((1,), (1,)), ((), ())), preferred_element_type=jnp.float32
        )
        grad_scores = probs * (grad_probs - jnp.sum(probs * grad_probs, axis=-1, keepdims=True))
        grad_scores = grad_scores.astype(jnp.bfloat16)
        grad_keys = (
            lax.dot_general(
                grad_scores, q, (((0,), (0,)), ((), ())), preferred_element_type=jnp.float32
            )
            * factor
        )
        acc_ref[first, :, kcols] += grad_keys[:NBR_LEN]
        acc_ref[second, :, kcols] += grad_keys[NBR_LEN:]
        acc_ref[first, :, vcols] += grad_values[:NBR_LEN]
        acc_ref[second, :, vcols] += grad_values[NBR_LEN:]

    @pl.when(span == pl.num_programs(0) - 1)
    def _():
        out_ref[...] = acc_ref[...].astype(out_ref.dtype)


def attention(owners, picks, queries, everyone, grad_attended, owner_count):
    rows, width = queries.shape
    spans = rows // SPAN
    heads = width // HD
    kv_width = everyone.shape[2]
    grid_spec = pltpu.PrefetchScalarGridSpec(
        num_scalar_prefetch=2,
        grid=(spans,),
        in_specs=[
            pl.BlockSpec((SPAN, width), lambda c, o, n: (c, 0)),
            pl.BlockSpec((1, NBR_LEN, kv_width), lambda c, o, n: (n[2 * c], 0, 0)),
            pl.BlockSpec((1, NBR_LEN, kv_width), lambda c, o, n: (n[2 * c + 1], 0, 0)),
            pl.BlockSpec((SPAN, width), lambda c, o, n: (c, 0)),
        ],
        out_specs=[
            pl.BlockSpec((SPAN, width), lambda c, o, n: (c, 0)),
            pl.BlockSpec((owner_count, NBR_LEN, kv_width), lambda c, o, n: (0, 0, 0)),
        ],
        scratch_shapes=[pltpu.VMEM((owner_count, NBR_LEN, kv_width), jnp.float32)],
    )
    return pl.pallas_call(
        functools.partial(attention_kernel, heads),
        grid_spec=grid_spec,
        out_shape=[
            jax.ShapeDtypeStruct((rows, width), jnp.bfloat16),
            jax.ShapeDtypeStruct((owner_count, NBR_LEN, kv_width), jnp.bfloat16),
        ],
        compiler_params=pltpu.CompilerParams(
            dimension_semantics=("arbitrary",), vmem_limit_bytes=56 * 1024 * 1024
        ),
    )(owners, picks, queries, everyone, everyone, grad_attended)


def slot_sum_kernel(readers, select_ref, returned_ref, out_ref):
    for slot in range(NB_DEV):
        total = returned_ref[0].astype(jnp.float32) * select_ref[0, slot]
        for r in range(1, readers):
            total = total + returned_ref[r].astype(jnp.float32) * select_ref[r, slot]
        out_ref[slot] = total.astype(out_ref.dtype)


def slot_sum(select, returned):
    readers, length, width = returned.shape
    tile = 256
    return pl.pallas_call(
        functools.partial(slot_sum_kernel, readers),
        grid=(width // tile,),
        in_specs=[
            pl.BlockSpec(memory_space=pltpu.SMEM),
            pl.BlockSpec((readers, length, tile), lambda j: (0, 0, j)),
        ],
        out_specs=pl.BlockSpec((NB_DEV, length, tile), lambda j: (0, 0, j)),
        out_shape=jax.ShapeDtypeStruct((NB_DEV, length, width), jnp.bfloat16),
    )(select, returned)


def exchange_kernel(x_ref, y_ref, send_sems, recv_sems, local_sem):
    count = lax.axis_size("dp")
    me = lax.axis_index("dp")
    column = lax.axis_index("tensor")
    copies = []
    for step in range(1, count):
        peer = lax.rem(me + step, count)
        copy = pltpu.make_async_remote_copy(
            src_ref=x_ref.at[peer],
            dst_ref=y_ref.at[me],
            send_sem=send_sems.at[step],
            recv_sem=recv_sems.at[step],
            device_id=(peer, column),
            device_id_type=pl.DeviceIdType.MESH,
        )
        copy.start()
        copies.append(copy)
    own = pltpu.make_async_copy(x_ref.at[me], y_ref.at[me], local_sem)
    own.start()
    own.wait()
    for copy in copies:
        copy.wait()


def exchange(blocks):
    count = blocks.shape[0]
    return pl.pallas_call(
        exchange_kernel,
        in_specs=[pl.BlockSpec(memory_space=pl.ANY)],
        out_specs=pl.BlockSpec(memory_space=pl.ANY),
        out_shape=jax.ShapeDtypeStruct(blocks.shape, blocks.dtype),
        scratch_shapes=[
            pltpu.SemaphoreType.DMA((count,)),
            pltpu.SemaphoreType.DMA((count,)),
            pltpu.SemaphoreType.DMA,
        ],
        compiler_params=pltpu.CompilerParams(has_side_effects=True),
    )(blocks)


def local(kv_part, queries, w_out, d_out, nbr_owner, nbr_slot):
    dp_count = lax.axis_size("dp")
    reader = lax.axis_index("dp")
    head_width = w_out.shape[0]
    share_width = 2 * head_width
    span_count = queries.shape[0] // SPAN
    read_count = 2 * span_count
    shares = lax.psum_scatter(kv_part[0], "tensor", scatter_dimension=1, tiled=True)
    share_blocks = shares.reshape(NB_DEV, NBR_LEN, share_width)
    owner_ids = jnp.arange(dp_count, dtype=jnp.int32)
    slot_ids = jnp.arange(NB_DEV, dtype=jnp.int32)
    owner_hits = nbr_owner[:, :, None] == owner_ids[None, None, :]
    per_reader = owner_hits.reshape(dp_count, read_count, dp_count)
    reads_from = jnp.any(per_reader, axis=1)
    slot_from = jnp.max(jnp.where(per_reader, nbr_slot.reshape(dp_count, read_count, 1), 0), axis=1)
    my_owner = lax.dynamic_slice_in_dim(nbr_owner, reader * span_count, span_count, 0).reshape(
        read_count
    )
    my_slot = lax.dynamic_slice_in_dim(nbr_slot, reader * span_count, span_count, 0).reshape(
        read_count
    )
    serving = lax.dynamic_index_in_dim(reads_from, reader, 1, False)
    serving_slot = lax.dynamic_index_in_dim(slot_from, reader, 1, False)
    owner_select = ((serving_slot[:, None] == slot_ids[None, :]) & serving[:, None]).astype(
        jnp.float32
    )
    outgoing = jnp.take(share_blocks, serving_slot, axis=0, mode="clip")
    everyone = exchange(outgoing)
    picks = my_owner
    grad_attended = lax.dot_general(
        lax.all_gather(d_out, "tensor", axis=1, tiled=True),
        w_out,
        (((1,), (1,)), ((), ())),
        preferred_element_type=jnp.float32,
    ).astype(jnp.bfloat16)
    attended, per_owner = attention(my_owner, picks, queries, everyone, grad_attended, dp_count)
    partial_out = jnp.dot(attended, w_out, preferred_element_type=jnp.float32)
    mixed = lax.psum_scatter(
        partial_out.astype(jnp.bfloat16), "tensor", scatter_dimension=1, tiled=True
    )
    returned = exchange(per_owner)
    owner_grad = slot_sum(owner_select, returned)
    d_kv = owner_grad.reshape(NB_DEV * NBR_LEN, share_width)
    return (mixed, d_kv)


def solution(mesh):
    placed = (
        P("tensor", "dp", None),
        P("dp", "tensor"),
        P("tensor", None),
        P("dp", "tensor"),
        P(),
        P(),
    )
    return jax.shard_map(
        local,
        mesh=mesh,
        in_specs=placed,
        out_specs=(P("dp", "tensor"), P("dp", "tensor")),
        check_vma=False,
    )
```

```python
import functools

import jax
import jax.numpy as jnp
from jax import lax
from jax.experimental import pallas as pl
from jax.experimental.pallas import tpu as pltpu
from jax.sharding import PartitionSpec as P

HD = 128
SPAN = 64
NBR_LEN = 128
NB_DEV = 2


def attention_kernel(heads, owner_ref, pick_ref, q_ref, first_ref, second_ref, g_ref, att_ref, out_ref, acc_ref):
    factor = HD ** (-0.5)
    span = pl.program_id(0)

    @pl.when(span == 0)
    def _():
        acc_ref[...] = jnp.zeros_like(acc_ref)

    first = owner_ref[2 * span]
    second = owner_ref[2 * span + 1]
    for h in range(heads):
        cols = slice(h * HD, (h + 1) * HD)
        kcols = slice(2 * h * HD, 2 * h * HD + HD)
        vcols = slice(2 * h * HD + HD, 2 * (h + 1) * HD)
        q = q_ref[:, cols]
        g = g_ref[:, cols]
        k = jnp.concatenate([first_ref[0, :, kcols], second_ref[0, :, kcols]], axis=0)
        v = jnp.concatenate([first_ref[0, :, vcols], second_ref[0, :, vcols]], axis=0)
        scores = (
            lax.dot_general(q, k, (((1,), (1,)), ((), ())), preferred_element_type=jnp.float32)
            * factor
        )
        top = jnp.max(scores, axis=-1, keepdims=True)
        expo = jnp.exp(scores - top)
        probs = expo / jnp.sum(expo, axis=-1, keepdims=True)
        probs_low = probs.astype(jnp.bfloat16)
        attended = jnp.dot(probs_low, v, preferred_element_type=jnp.float32)
        att_ref[:, cols] = attended.astype(att_ref.dtype)
        grad_values = lax.dot_general(
            probs_low, g, (((0,), (0,)), ((), ())), preferred_element_type=jnp.float32
        )
        grad_probs = lax.dot_general(
            g, v, (((1,), (1,)), ((), ())), preferred_element_type=jnp.float32
        )
        grad_scores = probs * (grad_probs - jnp.sum(probs * grad_probs, axis=-1, keepdims=True))
        grad_scores = grad_scores.astype(jnp.bfloat16)
        grad_keys = (
            lax.dot_general(
                grad_scores, q, (((0,), (0,)), ((), ())), preferred_element_type=jnp.float32
            )
            * factor
        )
        acc_ref[first, :, kcols] += grad_keys[:NBR_LEN]
        acc_ref[second, :, kcols] += grad_keys[NBR_LEN:]
        acc_ref[first, :, vcols] += grad_values[:NBR_LEN]
        acc_ref[second, :, vcols] += grad_values[NBR_LEN:]

    @pl.when(span == pl.num_programs(0) - 1)
    def _():
        out_ref[...] = acc_ref[...].astype(out_ref.dtype)


def attention(owners, picks, queries, everyone, grad_attended, owner_count):
    rows, width = queries.shape
    spans = rows // SPAN
    heads = width // HD
    kv_width = everyone.shape[2]
    grid_spec = pltpu.PrefetchScalarGridSpec(
        num_scalar_prefetch=2,
        grid=(spans,),
        in_specs=[
            pl.BlockSpec((SPAN, width), lambda c, o, n: (c, 0)),
            pl.BlockSpec((1, NBR_LEN, kv_width), lambda c, o, n: (n[2 * c], 0, 0)),
            pl.BlockSpec((1, NBR_LEN, kv_width), lambda c, o, n: (n[2 * c + 1], 0, 0)),
            pl.BlockSpec((SPAN, width), lambda c, o, n: (c, 0)),
        ],
        out_specs=[
            pl.BlockSpec((SPAN, width), lambda c, o, n: (c, 0)),
            pl.BlockSpec((owner_count, NBR_LEN, kv_width), lambda c, o, n: (0, 0, 0)),
        ],
        scratch_shapes=[pltpu.VMEM((owner_count, NBR_LEN, kv_width), jnp.float32)],
    )
    return pl.pallas_call(
        functools.partial(attention_kernel, heads),
        grid_spec=grid_spec,
        out_shape=[
            jax.ShapeDtypeStruct((rows, width), jnp.bfloat16),
            jax.ShapeDtypeStruct((owner_count, NBR_LEN, kv_width), jnp.bfloat16),
        ],
        compiler_params=pltpu.CompilerParams(
            dimension_semantics=("arbitrary",), vmem_limit_bytes=56 * 1024 * 1024
        ),
    )(owners, picks, queries, everyone, everyone, grad_attended)


def slot_sum_kernel(readers, select_ref, returned_ref, out_ref):
    for slot in range(NB_DEV):
        total = returned_ref[0].astype(jnp.float32) * select_ref[0, slot]
        for r in range(1, readers):
            total = total + returned_ref[r].astype(jnp.float32) * select_ref[r, slot]
        out_ref[slot] = total.astype(out_ref.dtype)


def slot_sum(select, returned):
    readers, length, width = returned.shape
    tile = 256
    return pl.pallas_call(
        functools.partial(slot_sum_kernel, readers),
        grid=(width // tile,),
        in_specs=[
            pl.BlockSpec(memory_space=pltpu.SMEM),
            pl.BlockSpec((readers, length, tile), lambda j: (0, 0, j)),
        ],
        out_specs=pl.BlockSpec((NB_DEV, length, tile), lambda j: (0, 0, j)),
        out_shape=jax.ShapeDtypeStruct((NB_DEV, length, width), jnp.bfloat16),
    )(select, returned)


def local(kv_part, queries, w_out, d_out, nbr_owner, nbr_slot):
    dp_count = lax.axis_size("dp")
    reader = lax.axis_index("dp")
    head_width = w_out.shape[0]
    share_width = 2 * head_width
    span_count = queries.shape[0] // SPAN
    read_count = 2 * span_count
    shares = lax.psum_scatter(kv_part[0], "tensor", scatter_dimension=1, tiled=True)
    share_blocks = shares.reshape(NB_DEV, NBR_LEN, share_width)
    owner_ids = jnp.arange(dp_count, dtype=jnp.int32)
    slot_ids = jnp.arange(NB_DEV, dtype=jnp.int32)
    owner_hits = nbr_owner[:, :, None] == owner_ids[None, None, :]
    per_reader = owner_hits.reshape(dp_count, read_count, dp_count)
    reads_from = jnp.any(per_reader, axis=1)
    slot_from = jnp.max(jnp.where(per_reader, nbr_slot.reshape(dp_count, read_count, 1), 0), axis=1)
    my_owner = lax.dynamic_slice_in_dim(nbr_owner, reader * span_count, span_count, 0).reshape(
        read_count
    )
    my_slot = lax.dynamic_slice_in_dim(nbr_slot, reader * span_count, span_count, 0).reshape(
        read_count
    )
    serving = lax.dynamic_index_in_dim(reads_from, reader, 1, False)
    serving_slot = lax.dynamic_index_in_dim(slot_from, reader, 1, False)
    owner_select = ((serving_slot[:, None] == slot_ids[None, :]) & serving[:, None]).astype(
        jnp.float32
    )
    everyone = lax.all_gather(share_blocks, "dp", axis=0, tiled=True)
    picks = my_owner * NB_DEV + my_slot
    tensor_count = lax.axis_size("tensor")
    column = lax.axis_index("tensor")
    direction = 1 - 2 * (column % 2)
    ring = [(t, (t + 2 * (1 - 2 * (t % 2))) % tensor_count) for t in range(tensor_count)]
    swap = [(t, t ^ 1) for t in range(tensor_count)]
    hops = tensor_count // 2
    mine = [d_out]
    for _ in range(hops - 1):
        mine.append(lax.ppermute(mine[-1], "tensor", ring))
    theirs = [lax.ppermute(block, "tensor", swap) for block in mine]
    steps = jnp.arange(hops, dtype=jnp.int32)
    slot_block = jnp.concatenate(
        [
            (column - 2 * direction * steps) % tensor_count,
            ((column ^ 1) + 2 * direction * steps) % tensor_count,
        ]
    )
    w_slots = jnp.take(
        w_out.reshape(head_width, tensor_count, d_out.shape[1]), slot_block, axis=1, mode="clip"
    )
    grad_attended = jnp.einsum(
        "tqc,htc->qh",
        jnp.stack(mine + theirs),
        w_slots,
        preferred_element_type=jnp.float32,
    ).astype(jnp.bfloat16)
    attended, per_owner = attention(my_owner, picks, queries, everyone, grad_attended, dp_count)
    partial_out = jnp.dot(attended, w_out, preferred_element_type=jnp.float32)
    mixed = lax.psum_scatter(
        partial_out.astype(jnp.bfloat16), "tensor", scatter_dimension=1, tiled=True
    )
    returned = lax.all_to_all(per_owner, "dp", split_axis=0, concat_axis=0, tiled=True)
    owner_grad = slot_sum(owner_select, returned)
    d_kv = owner_grad.reshape(NB_DEV * NBR_LEN, share_width)
    return (mixed, d_kv)


def solution(mesh):
    placed = (
        P("tensor", "dp", None),
        P("dp", "tensor"),
        P("tensor", None),
        P("dp", "tensor"),
        P(),
        P(),
    )
    return jax.shard_map(
        local,
        mesh=mesh,
        in_specs=placed,
        out_specs=(P("dp", "tensor"), P("dp", "tensor")),
        check_vma=False,
    )
```

```python
import functools

import jax
import jax.numpy as jnp
from jax import lax
from jax.experimental import pallas as pl
from jax.experimental.pallas import tpu as pltpu
from jax.sharding import PartitionSpec as P

HD = 128
SPAN = 64
NBR_LEN = 128
NB_DEV = 2


def attention_kernel(heads, owner_ref, pick_ref, q_ref, first_ref, second_ref, g_ref, att_ref, out_ref, acc_ref):
    factor = HD ** (-0.5)
    span = pl.program_id(0)

    @pl.when(span == 0)
    def _():
        acc_ref[...] = jnp.zeros_like(acc_ref)

    first = owner_ref[2 * span]
    second = owner_ref[2 * span + 1]
    for h in range(heads):
        cols = slice(h * HD, (h + 1) * HD)
        kcols = slice(2 * h * HD, 2 * h * HD + HD)
        vcols = slice(2 * h * HD + HD, 2 * (h + 1) * HD)
        q = q_ref[:, cols]
        g = g_ref[:, cols]
        k = jnp.concatenate([first_ref[0, :, kcols], second_ref[0, :, kcols]], axis=0)
        v = jnp.concatenate([first_ref[0, :, vcols], second_ref[0, :, vcols]], axis=0)
        scores = (
            lax.dot_general(q, k, (((1,), (1,)), ((), ())), preferred_element_type=jnp.float32)
            * factor
        )
        top = jnp.max(scores, axis=-1, keepdims=True)
        expo = jnp.exp(scores - top)
        probs = expo / jnp.sum(expo, axis=-1, keepdims=True)
        probs_low = probs.astype(jnp.bfloat16)
        attended = jnp.dot(probs_low, v, preferred_element_type=jnp.float32)
        att_ref[:, cols] = attended.astype(att_ref.dtype)
        grad_values = lax.dot_general(
            probs_low, g, (((0,), (0,)), ((), ())), preferred_element_type=jnp.float32
        )
        grad_probs = lax.dot_general(
            g, v, (((1,), (1,)), ((), ())), preferred_element_type=jnp.float32
        )
        grad_scores = probs * (grad_probs - jnp.sum(probs * grad_probs, axis=-1, keepdims=True))
        grad_scores = grad_scores.astype(jnp.bfloat16)
        grad_keys = (
            lax.dot_general(
                grad_scores, q, (((0,), (0,)), ((), ())), preferred_element_type=jnp.float32
            )
            * factor
        )
        acc_ref[first, :, kcols] += grad_keys[:NBR_LEN]
        acc_ref[second, :, kcols] += grad_keys[NBR_LEN:]
        acc_ref[first, :, vcols] += grad_values[:NBR_LEN]
        acc_ref[second, :, vcols] += grad_values[NBR_LEN:]

    @pl.when(span == pl.num_programs(0) - 1)
    def _():
        out_ref[...] = acc_ref[...].astype(out_ref.dtype)


def attention(owners, picks, queries, everyone, grad_attended, owner_count):
    rows, width = queries.shape
    spans = rows // SPAN
    heads = width // HD
    kv_width = everyone.shape[2]
    grid_spec = pltpu.PrefetchScalarGridSpec(
        num_scalar_prefetch=2,
        grid=(spans,),
        in_specs=[
            pl.BlockSpec((SPAN, width), lambda c, o, n: (c, 0)),
            pl.BlockSpec((1, NBR_LEN, kv_width), lambda c, o, n: (n[2 * c], 0, 0)),
            pl.BlockSpec((1, NBR_LEN, kv_width), lambda c, o, n: (n[2 * c + 1], 0, 0)),
            pl.BlockSpec((SPAN, width), lambda c, o, n: (c, 0)),
        ],
        out_specs=[
            pl.BlockSpec((SPAN, width), lambda c, o, n: (c, 0)),
            pl.BlockSpec((owner_count, NBR_LEN, kv_width), lambda c, o, n: (0, 0, 0)),
        ],
        scratch_shapes=[pltpu.VMEM((owner_count, NBR_LEN, kv_width), jnp.float32)],
    )
    return pl.pallas_call(
        functools.partial(attention_kernel, heads),
        grid_spec=grid_spec,
        out_shape=[
            jax.ShapeDtypeStruct((rows, width), jnp.bfloat16),
            jax.ShapeDtypeStruct((owner_count, NBR_LEN, kv_width), jnp.bfloat16),
        ],
        compiler_params=pltpu.CompilerParams(
            dimension_semantics=("arbitrary",), vmem_limit_bytes=56 * 1024 * 1024
        ),
    )(owners, picks, queries, everyone, everyone, grad_attended)


def local(kv_part, queries, w_out, d_out, nbr_owner, nbr_slot):
    dp_count = lax.axis_size("dp")
    reader = lax.axis_index("dp")
    head_width = w_out.shape[0]
    share_width = 2 * head_width
    span_count = queries.shape[0] // SPAN
    read_count = 2 * span_count
    shares = lax.psum_scatter(kv_part[0], "tensor", scatter_dimension=1, tiled=True)
    share_blocks = shares.reshape(NB_DEV, NBR_LEN, share_width)
    owner_ids = jnp.arange(dp_count, dtype=jnp.int32)
    slot_ids = jnp.arange(NB_DEV, dtype=jnp.int32)
    owner_hits = nbr_owner[:, :, None] == owner_ids[None, None, :]
    per_reader = owner_hits.reshape(dp_count, read_count, dp_count)
    slot_from = jnp.max(jnp.where(per_reader, nbr_slot.reshape(dp_count, read_count, 1), 0), axis=1)
    my_owner = lax.dynamic_slice_in_dim(nbr_owner, reader * span_count, span_count, 0).reshape(
        read_count
    )
    my_slot = lax.dynamic_slice_in_dim(nbr_slot, reader * span_count, span_count, 0).reshape(
        read_count
    )
    everyone = lax.all_gather(share_blocks, "dp", axis=0, tiled=True)
    picks = my_owner * NB_DEV + my_slot
    tensor_count = lax.axis_size("tensor")
    column = lax.axis_index("tensor")
    direction = 1 - 2 * (column % 2)
    ring = [(t, (t + 2 * (1 - 2 * (t % 2))) % tensor_count) for t in range(tensor_count)]
    swap = [(t, t ^ 1) for t in range(tensor_count)]
    hops = tensor_count // 2
    mine = [d_out]
    for _ in range(hops - 1):
        mine.append(lax.ppermute(mine[-1], "tensor", ring))
    theirs = [lax.ppermute(block, "tensor", swap) for block in mine]
    steps = jnp.arange(hops, dtype=jnp.int32)
    slot_block = jnp.concatenate(
        [
            (column - 2 * direction * steps) % tensor_count,
            ((column ^ 1) + 2 * direction * steps) % tensor_count,
        ]
    )
    w_slots = jnp.take(
        w_out.reshape(head_width, tensor_count, d_out.shape[1]), slot_block, axis=1, mode="clip"
    )
    grad_attended = jnp.einsum(
        "tqc,htc->qh",
        jnp.stack(mine + theirs),
        w_slots,
        preferred_element_type=jnp.float32,
    ).astype(jnp.bfloat16)
    attended, per_owner = attention(my_owner, picks, queries, everyone, grad_attended, dp_count)
    partial_out = jnp.dot(attended, w_out, preferred_element_type=jnp.float32).astype(
        jnp.bfloat16
    )
    slot_mask = lax.dynamic_index_in_dim(slot_from, reader, 0, False)[:, None] == slot_ids[None, :]
    expanded = jnp.where(slot_mask[:, :, None, None], per_owner[:, None], jnp.zeros_like(per_owner[:, None]))
    owner_grad = lax.psum_scatter(
        expanded.reshape(dp_count * NB_DEV, NBR_LEN, share_width),
        "dp",
        scatter_dimension=0,
        tiled=True,
    )
    d_kv = owner_grad.reshape(NB_DEV * NBR_LEN, share_width)
    cycle = list(range(0, tensor_count, 2)) + list(range(tensor_count - 1, 0, -2))
    position_of = [cycle.index(t) for t in range(tensor_count)]
    rightward = [(cycle[p], cycle[(p + 1) % tensor_count]) for p in range(tensor_count)]
    leftward = [(cycle[p], cycle[(p - 1) % tensor_count]) for p in range(tensor_count)]
    cycle_table = jnp.array(cycle, dtype=jnp.int32)
    position = jnp.array(position_of, dtype=jnp.int32)[column]
    block_width = partial_out.shape[1] // tensor_count
    half = block_width // 2

    def piece(offset, part):
        block = cycle_table[(position + offset) % tensor_count]
        return lax.dynamic_slice_in_dim(partial_out, block * block_width + part * half, half, 1)

    halves = []
    for part, perm, sign in ((0, rightward, -1), (1, leftward, 1)):
        acc = piece(sign, part)
        for step in range(tensor_count - 1):
            arrived = lax.ppermute(acc, "tensor", perm)
            acc = (
                arrived.astype(jnp.float32) + piece(sign * (step + 2), part).astype(jnp.float32)
            ).astype(jnp.bfloat16)
        halves.append(acc)
    mixed = jnp.concatenate(halves, axis=1)
    return (mixed, d_kv)


def solution(mesh):
    placed = (
        P("tensor", "dp", None),
        P("dp", "tensor"),
        P("tensor", None),
        P("dp", "tensor"),
        P(),
        P(),
    )
    return jax.shard_map(
        local,
        mesh=mesh,
        in_specs=placed,
        out_specs=(P("dp", "tensor"), P("dp", "tensor")),
        check_vma=False,
    )
```

```python
import functools

import jax
import jax.numpy as jnp
from jax import lax
from jax.experimental import pallas as pl
from jax.experimental.pallas import tpu as pltpu
from jax.sharding import PartitionSpec as P

HD = 128
SPAN = 64
NBR_LEN = 128
NB_DEV = 2


def attention_kernel(heads, owner_ref, pick_ref, q_ref, first_ref, second_ref, g_ref, *rest):
    att_ref, out_ref, acc_ref = rest[-3:]
    factor = HD ** (-0.5)
    span = pl.program_id(0)

    @pl.when(span == 0)
    def _():
        acc_ref[...] = jnp.zeros_like(acc_ref)

    first = owner_ref[2 * span]
    second = owner_ref[2 * span + 1]
    for h in range(heads):
        cols = slice(h * HD, (h + 1) * HD)
        kcols = slice(2 * h * HD, 2 * h * HD + HD)
        vcols = slice(2 * h * HD + HD, 2 * (h + 1) * HD)
        q = q_ref[:, cols]
        g = g_ref[:, cols]
        k = jnp.concatenate([first_ref[0, :, kcols], second_ref[0, :, kcols]], axis=0)
        v = jnp.concatenate([first_ref[0, :, vcols], second_ref[0, :, vcols]], axis=0)
        scores = (
            lax.dot_general(q, k, (((1,), (1,)), ((), ())), preferred_element_type=jnp.float32)
            * factor
        )
        top = jnp.max(scores, axis=-1, keepdims=True)
        expo = jnp.exp(scores - top)
        probs = expo / jnp.sum(expo, axis=-1, keepdims=True)
        probs_low = probs.astype(jnp.bfloat16)
        attended = jnp.dot(probs_low, v, preferred_element_type=jnp.float32)
        att_ref[:, cols] = attended.astype(att_ref.dtype)
        grad_values = lax.dot_general(
            probs_low, g, (((0,), (0,)), ((), ())), preferred_element_type=jnp.float32
        )
        grad_probs = lax.dot_general(
            g, v, (((1,), (1,)), ((), ())), preferred_element_type=jnp.float32
        )
        grad_scores = probs * (grad_probs - jnp.sum(probs * grad_probs, axis=-1, keepdims=True))
        grad_scores = grad_scores.astype(jnp.bfloat16)
        grad_keys = (
            lax.dot_general(
                grad_scores, q, (((0,), (0,)), ((), ())), preferred_element_type=jnp.float32
            )
            * factor
        )
        acc_ref[first, :, kcols] += grad_keys[:NBR_LEN]
        acc_ref[second, :, kcols] += grad_keys[NBR_LEN:]
        acc_ref[first, :, vcols] += grad_values[:NBR_LEN]
        acc_ref[second, :, vcols] += grad_values[NBR_LEN:]

    @pl.when(span == pl.num_programs(0) - 1)
    def _():
        out_ref[...] = acc_ref[...].astype(out_ref.dtype)


def attention(owners, picks, queries, everyone, grad_attended, owner_count, chunk, chunks, prior):
    rows, full_width = queries.shape
    spans = rows // SPAN
    kv_width = everyone.shape[2]
    width = kv_width // 2
    heads = width // HD
    in_specs = [
        pl.BlockSpec((SPAN, width), lambda c, o, n: (c, chunk)),
        pl.BlockSpec((1, NBR_LEN, kv_width), lambda c, o, n: (n[2 * c], 0, 0)),
        pl.BlockSpec((1, NBR_LEN, kv_width), lambda c, o, n: (n[2 * c + 1], 0, 0)),
        pl.BlockSpec((SPAN, width), lambda c, o, n: (c, chunk)),
    ]
    operands = [owners, picks, queries, everyone, everyone, grad_attended]
    aliases = {}
    if prior is not None:
        in_specs += [pl.BlockSpec(memory_space=pl.ANY)] * 2
        operands += list(prior)
        aliases = {6: 0, 7: 1}
    grid_spec = pltpu.PrefetchScalarGridSpec(
        num_scalar_prefetch=2,
        grid=(spans,),
        in_specs=in_specs,
        out_specs=[
            pl.BlockSpec((SPAN, width), lambda c, o, n: (c, chunk)),
            pl.BlockSpec((owner_count, NBR_LEN, kv_width), lambda c, o, n: (0, 0, chunk)),
        ],
        scratch_shapes=[pltpu.VMEM((owner_count, NBR_LEN, kv_width), jnp.float32)],
    )
    return pl.pallas_call(
        functools.partial(attention_kernel, heads),
        grid_spec=grid_spec,
        out_shape=[
            jax.ShapeDtypeStruct((rows, full_width), jnp.bfloat16),
            jax.ShapeDtypeStruct((owner_count, NBR_LEN, kv_width * chunks), jnp.bfloat16),
        ],
        input_output_aliases=aliases,
        compiler_params=pltpu.CompilerParams(
            dimension_semantics=("arbitrary",), vmem_limit_bytes=48 * 1024 * 1024
        ),
    )(*operands)


def slot_sum_kernel(readers, select_ref, returned_ref, out_ref):
    for slot in range(NB_DEV):
        total = returned_ref[0].astype(jnp.float32) * select_ref[0, slot]
        for r in range(1, readers):
            total = total + returned_ref[r].astype(jnp.float32) * select_ref[r, slot]
        out_ref[slot] = total.astype(out_ref.dtype)


def slot_sum(select, returned):
    readers, length, width = returned.shape
    tile = 256
    return pl.pallas_call(
        functools.partial(slot_sum_kernel, readers),
        grid=(width // tile,),
        in_specs=[
            pl.BlockSpec(memory_space=pltpu.SMEM),
            pl.BlockSpec((readers, length, tile), lambda j: (0, 0, j)),
        ],
        out_specs=pl.BlockSpec((NB_DEV, length, tile), lambda j: (0, 0, j)),
        out_shape=jax.ShapeDtypeStruct((NB_DEV, length, width), jnp.bfloat16),
    )(select, returned)


def local(kv_part, queries, w_out, d_out, nbr_owner, nbr_slot):
    dp_count = lax.axis_size("dp")
    reader = lax.axis_index("dp")
    head_width = w_out.shape[0]
    share_width = 2 * head_width
    span_count = queries.shape[0] // SPAN
    read_count = 2 * span_count
    shares = lax.psum_scatter(kv_part[0], "tensor", scatter_dimension=1, tiled=True)
    share_blocks = shares.reshape(NB_DEV, NBR_LEN, share_width)
    owner_ids = jnp.arange(dp_count, dtype=jnp.int32)
    slot_ids = jnp.arange(NB_DEV, dtype=jnp.int32)
    owner_hits = nbr_owner[:, :, None] == owner_ids[None, None, :]
    per_reader = owner_hits.reshape(dp_count, read_count, dp_count)
    reads_from = jnp.any(per_reader, axis=1)
    slot_from = jnp.max(jnp.where(per_reader, nbr_slot.reshape(dp_count, read_count, 1), 0), axis=1)
    my_owner = lax.dynamic_slice_in_dim(nbr_owner, reader * span_count, span_count, 0).reshape(
        read_count
    )
    my_slot = lax.dynamic_slice_in_dim(nbr_slot, reader * span_count, span_count, 0).reshape(
        read_count
    )
    serving = lax.dynamic_index_in_dim(reads_from, reader, 1, False)
    serving_slot = lax.dynamic_index_in_dim(slot_from, reader, 1, False)
    owner_select = ((serving_slot[:, None] == slot_ids[None, :]) & serving[:, None]).astype(
        jnp.float32
    )
    picks = my_owner * NB_DEV + my_slot
    tensor_count = lax.axis_size("tensor")
    column = lax.axis_index("tensor")
    direction = 1 - 2 * (column % 2)
    ring = [(t, (t + 2 * (1 - 2 * (t % 2))) % tensor_count) for t in range(tensor_count)]
    swap = [(t, t ^ 1) for t in range(tensor_count)]
    hops = tensor_count // 2
    mine = [d_out]
    for _ in range(hops - 1):
        mine.append(lax.ppermute(mine[-1], "tensor", ring))
    theirs = [lax.ppermute(block, "tensor", swap) for block in mine]
    steps = jnp.arange(hops, dtype=jnp.int32)
    slot_block = jnp.concatenate(
        [
            (column - 2 * direction * steps) % tensor_count,
            ((column ^ 1) + 2 * direction * steps) % tensor_count,
        ]
    )
    block_slot = jnp.argmax(
        slot_block[None, :] == jnp.arange(tensor_count, dtype=jnp.int32)[:, None], axis=1
    )
    ordered = jnp.take(jnp.stack(mine + theirs), block_slot, axis=0, mode="clip")
    grad_attended = jnp.einsum(
        "tqc,htc->qh",
        ordered,
        w_out.reshape(head_width, tensor_count, d_out.shape[1]),
        preferred_element_type=jnp.float32,
    ).astype(jnp.bfloat16)
    chunks = 2
    chunk_width = share_width // chunks
    outputs = None
    for chunk in range(chunks):
        everyone = lax.all_gather(
            share_blocks[:, :, chunk * chunk_width:(chunk + 1) * chunk_width],
            "dp",
            axis=0,
            tiled=True,
        )
        outputs = attention(
            my_owner, picks, queries, everyone, grad_attended, dp_count, chunk, chunks, outputs
        )
    attended, per_owner = outputs
    partial_out = jnp.dot(attended, w_out, preferred_element_type=jnp.float32)
    mixed = lax.psum_scatter(
        partial_out.astype(jnp.bfloat16), "tensor", scatter_dimension=1, tiled=True
    )
    returned = lax.all_to_all(per_owner, "dp", split_axis=0, concat_axis=0, tiled=True)
    owner_grad = slot_sum(owner_select, returned)
    d_kv = owner_grad.reshape(NB_DEV * NBR_LEN, share_width)
    return (mixed, d_kv)


def solution(mesh):
    placed = (
        P("tensor", "dp", None),
        P("dp", "tensor"),
        P("tensor", None),
        P("dp", "tensor"),
        P(),
        P(),
    )
    return jax.shard_map(
        local,
        mesh=mesh,
        in_specs=placed,
        out_specs=(P("dp", "tensor"), P("dp", "tensor")),
        check_vma=False,
    )
```

```python
import functools

import jax
import jax.numpy as jnp
from jax import lax
from jax.experimental import pallas as pl
from jax.experimental.pallas import tpu as pltpu
from jax.sharding import PartitionSpec as P

HD = 128
SPAN = 64
NBR_LEN = 128
NB_DEV = 2


def attention_kernel(heads, owner_ref, pick_ref, q_ref, first_ref, second_ref, g_ref, att_ref, out_ref, acc_ref):
    factor = HD ** (-0.5)
    span = pl.program_id(0)

    @pl.when(span == 0)
    def _():
        acc_ref[...] = jnp.zeros_like(acc_ref)

    owners = (owner_ref[2 * span], owner_ref[2 * span + 1])
    sources = (first_ref, second_ref)
    nt = (((1,), (1,)), ((), ()))
    tn = (((0,), (0,)), ((), ()))
    for h in range(heads):
        cols = slice(h * HD, (h + 1) * HD)
        kcols = slice(2 * h * HD, 2 * h * HD + HD)
        vcols = slice(2 * h * HD + HD, 2 * (h + 1) * HD)
        q = q_ref[:, cols]
        g = g_ref[:, cols]
        keys = [src[0, :, kcols] for src in sources]
        values = [src[0, :, vcols] for src in sources]
        scores = [
            lax.dot_general(q, k, nt, preferred_element_type=jnp.float32) * factor for k in keys
        ]
        top = jnp.maximum(
            jnp.max(scores[0], axis=-1, keepdims=True), jnp.max(scores[1], axis=-1, keepdims=True)
        )
        expo = [jnp.exp(s - top) for s in scores]
        total = jnp.sum(expo[0], axis=-1, keepdims=True) + jnp.sum(expo[1], axis=-1, keepdims=True)
        probs = [e / total for e in expo]
        probs_low = [p.astype(jnp.bfloat16) for p in probs]
        attended = jnp.dot(probs_low[0], values[0], preferred_element_type=jnp.float32) + jnp.dot(
            probs_low[1], values[1], preferred_element_type=jnp.float32
        )
        att_ref[:, cols] = attended.astype(att_ref.dtype)
        grad_probs = [lax.dot_general(g, v, nt, preferred_element_type=jnp.float32) for v in values]
        inner = jnp.sum(probs[0] * grad_probs[0], axis=-1, keepdims=True) + jnp.sum(
            probs[1] * grad_probs[1], axis=-1, keepdims=True
        )
        for j in range(2):
            grad_values = lax.dot_general(probs_low[j], g, tn, preferred_element_type=jnp.float32)
            grad_scores = (probs[j] * (grad_probs[j] - inner)).astype(jnp.bfloat16)
            grad_keys = (
                lax.dot_general(grad_scores, q, tn, preferred_element_type=jnp.float32) * factor
            )
            acc_ref[owners[j], :, kcols] += grad_keys
            acc_ref[owners[j], :, vcols] += grad_values

    @pl.when(span == pl.num_programs(0) - 1)
    def _():
        out_ref[...] = acc_ref[...].astype(out_ref.dtype)


def attention(owners, picks, queries, everyone, grad_attended, owner_count):
    rows, width = queries.shape
    spans = rows // SPAN
    heads = width // HD
    kv_width = everyone.shape[2]
    grid_spec = pltpu.PrefetchScalarGridSpec(
        num_scalar_prefetch=2,
        grid=(spans,),
        in_specs=[
            pl.BlockSpec((SPAN, width), lambda c, o, n: (c, 0)),
            pl.BlockSpec((1, NBR_LEN, kv_width), lambda c, o, n: (n[2 * c], 0, 0)),
            pl.BlockSpec((1, NBR_LEN, kv_width), lambda c, o, n: (n[2 * c + 1], 0, 0)),
            pl.BlockSpec((SPAN, width), lambda c, o, n: (c, 0)),
        ],
        out_specs=[
            pl.BlockSpec((SPAN, width), lambda c, o, n: (c, 0)),
            pl.BlockSpec((owner_count, NBR_LEN, kv_width), lambda c, o, n: (0, 0, 0)),
        ],
        scratch_shapes=[pltpu.VMEM((owner_count, NBR_LEN, kv_width), jnp.float32)],
    )
    return pl.pallas_call(
        functools.partial(attention_kernel, heads),
        grid_spec=grid_spec,
        out_shape=[
            jax.ShapeDtypeStruct((rows, width), jnp.bfloat16),
            jax.ShapeDtypeStruct((owner_count, NBR_LEN, kv_width), jnp.bfloat16),
        ],
        compiler_params=pltpu.CompilerParams(
            dimension_semantics=("arbitrary",), vmem_limit_bytes=56 * 1024 * 1024
        ),
    )(owners, picks, queries, everyone, everyone, grad_attended)


def slot_sum_kernel(readers, select_ref, returned_ref, out_ref):
    for slot in range(NB_DEV):
        total = returned_ref[0].astype(jnp.float32) * select_ref[0, slot]
        for r in range(1, readers):
            total = total + returned_ref[r].astype(jnp.float32) * select_ref[r, slot]
        out_ref[slot] = total.astype(out_ref.dtype)


def slot_sum(select, returned):
    readers, length, width = returned.shape
    tile = 768
    return pl.pallas_call(
        functools.partial(slot_sum_kernel, readers),
        grid=(width // tile,),
        in_specs=[
            pl.BlockSpec(memory_space=pltpu.SMEM),
            pl.BlockSpec((readers, length, tile), lambda j: (0, 0, j)),
        ],
        out_specs=pl.BlockSpec((NB_DEV, length, tile), lambda j: (0, 0, j)),
        out_shape=jax.ShapeDtypeStruct((NB_DEV, length, width), jnp.bfloat16),
    )(select, returned)


def local(kv_part, queries, w_out, d_out, nbr_owner, nbr_slot):
    dp_count = lax.axis_size("dp")
    reader = lax.axis_index("dp")
    head_width = w_out.shape[0]
    share_width = 2 * head_width
    span_count = queries.shape[0] // SPAN
    read_count = 2 * span_count
    shares = lax.psum_scatter(kv_part[0], "tensor", scatter_dimension=1, tiled=True)
    share_blocks = shares.reshape(NB_DEV, NBR_LEN, share_width)
    owner_ids = jnp.arange(dp_count, dtype=jnp.int32)
    slot_ids = jnp.arange(NB_DEV, dtype=jnp.int32)
    owner_hits = nbr_owner[:, :, None] == owner_ids[None, None, :]
    per_reader = owner_hits.reshape(dp_count, read_count, dp_count)
    reads_from = jnp.any(per_reader, axis=1)
    slot_from = jnp.max(jnp.where(per_reader, nbr_slot.reshape(dp_count, read_count, 1), 0), axis=1)
    my_owner = lax.dynamic_slice_in_dim(nbr_owner, reader * span_count, span_count, 0).reshape(
        read_count
    )
    my_slot = lax.dynamic_slice_in_dim(nbr_slot, reader * span_count, span_count, 0).reshape(
        read_count
    )
    serving = lax.dynamic_index_in_dim(reads_from, reader, 1, False)
    serving_slot = lax.dynamic_index_in_dim(slot_from, reader, 1, False)
    owner_select = ((serving_slot[:, None] == slot_ids[None, :]) & serving[:, None]).astype(
        jnp.float32
    )
    everyone = lax.all_gather(share_blocks, "dp", axis=0, tiled=True)
    picks = my_owner * NB_DEV + my_slot
    tensor_count = lax.axis_size("tensor")
    column = lax.axis_index("tensor")
    direction = 1 - 2 * (column % 2)
    ring = [(t, (t + 2 * (1 - 2 * (t % 2))) % tensor_count) for t in range(tensor_count)]
    swap = [(t, t ^ 1) for t in range(tensor_count)]
    hops = tensor_count // 2
    mine = [d_out]
    for _ in range(hops - 1):
        mine.append(lax.ppermute(mine[-1], "tensor", ring))
    theirs = [lax.ppermute(block, "tensor", swap) for block in mine]
    steps = jnp.arange(hops, dtype=jnp.int32)
    slot_block = jnp.concatenate(
        [
            (column - 2 * direction * steps) % tensor_count,
            ((column ^ 1) + 2 * direction * steps) % tensor_count,
        ]
    )
    block_slot = jnp.argmax(
        slot_block[None, :] == jnp.arange(tensor_count, dtype=jnp.int32)[:, None], axis=1
    )
    ordered = jnp.take(jnp.stack(mine + theirs), block_slot, axis=0, mode="clip")
    grad_attended = jnp.einsum(
        "tqc,htc->qh",
        ordered,
        w_out.reshape(head_width, tensor_count, d_out.shape[1]),
        preferred_element_type=jnp.float32,
    ).astype(jnp.bfloat16)
    attended, per_owner = attention(my_owner, picks, queries, everyone, grad_attended, dp_count)
    partial_out = jnp.dot(attended, w_out, preferred_element_type=jnp.float32)
    mixed = lax.psum_scatter(
        partial_out.astype(jnp.bfloat16), "tensor", scatter_dimension=1, tiled=True
    )
    returned = lax.all_to_all(per_owner, "dp", split_axis=0, concat_axis=0, tiled=True)
    owner_grad = slot_sum(owner_select, returned)
    d_kv = owner_grad.reshape(NB_DEV * NBR_LEN, share_width)
    return (mixed, d_kv)


def solution(mesh):
    placed = (
        P("tensor", "dp", None),
        P("dp", "tensor"),
        P("tensor", None),
        P("dp", "tensor"),
        P(),
        P(),
    )
    return jax.shard_map(
        local,
        mesh=mesh,
        in_specs=placed,
        out_specs=(P("dp", "tensor"), P("dp", "tensor")),
        check_vma=False,
    )
```

```python
import functools

import jax
import jax.numpy as jnp
from jax import lax
from jax.experimental import pallas as pl
from jax.experimental.pallas import tpu as pltpu
from jax.sharding import PartitionSpec as P

HD = 128
SPAN = 64
NBR_LEN = 128
NB_DEV = 2


def attention_kernel(heads, owner_ref, pick_ref, q_ref, first_ref, second_ref, g_ref, att_ref, out_ref, acc_ref):
    factor = HD ** (-0.5)
    span = pl.program_id(0)

    @pl.when(span == 0)
    def _():
        acc_ref[...] = jnp.zeros_like(acc_ref)

    first = owner_ref[2 * span]
    second = owner_ref[2 * span + 1]
    for h in range(heads):
        cols = slice(h * HD, (h + 1) * HD)
        kcols = slice(2 * h * HD, 2 * h * HD + HD)
        vcols = slice(2 * h * HD + HD, 2 * (h + 1) * HD)
        q = q_ref[:, cols]
        g = g_ref[:, cols]
        k = jnp.concatenate([first_ref[0, :, kcols], second_ref[0, :, kcols]], axis=0)
        v = jnp.concatenate([first_ref[0, :, vcols], second_ref[0, :, vcols]], axis=0)
        scores = (
            lax.dot_general(q, k, (((1,), (1,)), ((), ())), preferred_element_type=jnp.float32)
            * factor
        )
        top = jnp.max(scores, axis=-1, keepdims=True)
        expo = jnp.exp(scores - top)
        probs = expo / jnp.sum(expo, axis=-1, keepdims=True)
        probs_low = probs.astype(jnp.bfloat16)
        attended = jnp.dot(probs_low, v, preferred_element_type=jnp.float32)
        att_ref[:, cols] = attended.astype(att_ref.dtype)
        grad_values = lax.dot_general(
            probs_low, g, (((0,), (0,)), ((), ())), preferred_element_type=jnp.float32
        )
        grad_probs = lax.dot_general(
            g, v, (((1,), (1,)), ((), ())), preferred_element_type=jnp.float32
        )
        grad_scores = probs * (grad_probs - jnp.sum(probs * grad_probs, axis=-1, keepdims=True))
        grad_scores = grad_scores.astype(jnp.bfloat16)
        grad_keys = (
            lax.dot_general(
                grad_scores, q, (((0,), (0,)), ((), ())), preferred_element_type=jnp.float32
            )
            * factor
        )
        acc_ref[first, :, kcols] += grad_keys[:NBR_LEN]
        acc_ref[second, :, kcols] += grad_keys[NBR_LEN:]
        acc_ref[first, :, vcols] += grad_values[:NBR_LEN]
        acc_ref[second, :, vcols] += grad_values[NBR_LEN:]

    @pl.when(span == pl.num_programs(0) - 1)
    def _():
        out_ref[...] = acc_ref[...].astype(out_ref.dtype)


def attention(owners, picks, queries, everyone, grad_attended, owner_count):
    rows, width = queries.shape
    spans = rows // SPAN
    heads = width // HD
    kv_width = everyone.shape[2]
    grid_spec = pltpu.PrefetchScalarGridSpec(
        num_scalar_prefetch=2,
        grid=(spans,),
        in_specs=[
            pl.BlockSpec((SPAN, width), lambda c, o, n: (c, 0)),
            pl.BlockSpec((1, NBR_LEN, kv_width), lambda c, o, n: (n[2 * c], 0, 0)),
            pl.BlockSpec((1, NBR_LEN, kv_width), lambda c, o, n: (n[2 * c + 1], 0, 0)),
            pl.BlockSpec((SPAN, width), lambda c, o, n: (c, 0)),
        ],
        out_specs=[
            pl.BlockSpec((SPAN, width), lambda c, o, n: (c, 0)),
            pl.BlockSpec((owner_count, NBR_LEN, kv_width), lambda c, o, n: (0, 0, 0)),
        ],
        scratch_shapes=[pltpu.VMEM((owner_count, NBR_LEN, kv_width), jnp.float32)],
    )
    return pl.pallas_call(
        functools.partial(attention_kernel, heads),
        grid_spec=grid_spec,
        out_shape=[
            jax.ShapeDtypeStruct((rows, width), jnp.bfloat16),
            jax.ShapeDtypeStruct((owner_count, NBR_LEN, kv_width), jnp.bfloat16),
        ],
        compiler_params=pltpu.CompilerParams(
            dimension_semantics=("arbitrary",), vmem_limit_bytes=56 * 1024 * 1024
        ),
    )(owners, picks, queries, everyone, everyone, grad_attended)


def slot_sum_kernel(readers, select_ref, returned_ref, out_ref):
    for slot in range(NB_DEV):
        total = returned_ref[0].astype(jnp.float32) * select_ref[0, slot]
        for r in range(1, readers):
            total = total + returned_ref[r].astype(jnp.float32) * select_ref[r, slot]
        out_ref[slot] = total.astype(out_ref.dtype)


def slot_sum(select, returned):
    readers, length, width = returned.shape
    tile = 768
    return pl.pallas_call(
        functools.partial(slot_sum_kernel, readers),
        grid=(width // tile,),
        in_specs=[
            pl.BlockSpec(memory_space=pltpu.SMEM),
            pl.BlockSpec((readers, length, tile), lambda j: (0, 0, j)),
        ],
        out_specs=pl.BlockSpec((NB_DEV, length, tile), lambda j: (0, 0, j)),
        out_shape=jax.ShapeDtypeStruct((NB_DEV, length, width), jnp.bfloat16),
    )(select, returned)


def local(kv_part, queries, w_out, d_out, nbr_owner, nbr_slot):
    dp_count = lax.axis_size("dp")
    reader = lax.axis_index("dp")
    head_width = w_out.shape[0]
    share_width = 2 * head_width
    span_count = queries.shape[0] // SPAN
    read_count = 2 * span_count
    shares = lax.psum_scatter(kv_part[0], "tensor", scatter_dimension=1, tiled=True)
    share_blocks = shares.reshape(NB_DEV, NBR_LEN, share_width)
    owner_ids = jnp.arange(dp_count, dtype=jnp.int32)
    slot_ids = jnp.arange(NB_DEV, dtype=jnp.int32)
    owner_hits = nbr_owner[:, :, None] == owner_ids[None, None, :]
    per_reader = owner_hits.reshape(dp_count, read_count, dp_count)
    reads_from = jnp.any(per_reader, axis=1)
    slot_from = jnp.max(jnp.where(per_reader, nbr_slot.reshape(dp_count, read_count, 1), 0), axis=1)
    my_owner = lax.dynamic_slice_in_dim(nbr_owner, reader * span_count, span_count, 0).reshape(
        read_count
    )
    my_slot = lax.dynamic_slice_in_dim(nbr_slot, reader * span_count, span_count, 0).reshape(
        read_count
    )
    serving = lax.dynamic_index_in_dim(reads_from, reader, 1, False)
    serving_slot = lax.dynamic_index_in_dim(slot_from, reader, 1, False)
    owner_select = ((serving_slot[:, None] == slot_ids[None, :]) & serving[:, None]).astype(
        jnp.float32
    )
    everyone = lax.all_gather(share_blocks, "dp", axis=0, tiled=True)
    picks = my_owner * NB_DEV + my_slot
    tensor_count = lax.axis_size("tensor")
    column = lax.axis_index("tensor")
    direction = 1 - 2 * (column % 2)
    ring = [(t, (t + 2 * (1 - 2 * (t % 2))) % tensor_count) for t in range(tensor_count)]
    swap = [(t, t ^ 1) for t in range(tensor_count)]
    hops = tensor_count // 2
    mine = [d_out]
    for _ in range(hops - 1):
        mine.append(lax.ppermute(mine[-1], "tensor", ring))
    theirs = [lax.ppermute(block, "tensor", swap) for block in mine]
    steps = jnp.arange(hops, dtype=jnp.int32)
    slot_block = jnp.concatenate(
        [
            (column - 2 * direction * steps) % tensor_count,
            ((column ^ 1) + 2 * direction * steps) % tensor_count,
        ]
    )
    block_slot = jnp.argmax(
        slot_block[None, :] == jnp.arange(tensor_count, dtype=jnp.int32)[:, None], axis=1
    )
    ordered = jnp.take(jnp.stack(mine + theirs), block_slot, axis=0, mode="clip")
    grad_attended = jnp.einsum(
        "tqc,htc->qh",
        ordered,
        w_out.reshape(head_width, tensor_count, d_out.shape[1]),
        preferred_element_type=jnp.float32,
    ).astype(jnp.bfloat16)
    attended, per_owner = attention(my_owner, picks, queries, everyone, grad_attended, dp_count)
    partial_out = jnp.dot(attended, w_out, preferred_element_type=jnp.float32)
    mixed = lax.psum_scatter(
        partial_out.astype(jnp.bfloat16), "tensor", scatter_dimension=1, tiled=True
    )
    returned = lax.all_to_all(per_owner, "dp", split_axis=0, concat_axis=0, tiled=True)
    owner_grad = slot_sum(owner_select, returned)
    d_kv = owner_grad.reshape(NB_DEV * NBR_LEN, share_width)
    return (mixed, d_kv)


def solution(mesh):
    placed = (
        P("tensor", "dp", None),
        P("dp", "tensor"),
        P("tensor", None),
        P("dp", "tensor"),
        P(),
        P(),
    )
    return jax.shard_map(
        local,
        mesh=mesh,
        in_specs=placed,
        out_specs=(P("dp", "tensor"), P("dp", "tensor")),
        check_vma=False,
    )
```

```python
import functools

import jax
import jax.numpy as jnp
from jax import lax
from jax.experimental import pallas as pl
from jax.experimental.pallas import tpu as pltpu
from jax.sharding import PartitionSpec as P

HD = 128
SPAN = 64
NBR_LEN = 128
NB_DEV = 2


def attention_kernel(heads, per_step, owner_ref, pick_ref, q_ref, g_ref, *rest):
    kv_refs = rest[: 2 * per_step]
    att_ref, out_ref, acc_ref = rest[2 * per_step:]
    factor = HD ** (-0.5)
    step = pl.program_id(0)

    @pl.when(step == 0)
    def _():
        acc_ref[...] = jnp.zeros_like(acc_ref)

    for sub in range(per_step):
        first_ref, second_ref = kv_refs[2 * sub], kv_refs[2 * sub + 1]
        span = step * per_step + sub
        first = owner_ref[2 * span]
        second = owner_ref[2 * span + 1]
        rows = slice(sub * SPAN, (sub + 1) * SPAN)
        for h in range(heads):
            cols = slice(h * HD, (h + 1) * HD)
            kcols = slice(2 * h * HD, 2 * h * HD + HD)
            vcols = slice(2 * h * HD + HD, 2 * (h + 1) * HD)
            q = q_ref[rows, cols]
            g = g_ref[rows, cols]
            k = jnp.concatenate([first_ref[0, :, kcols], second_ref[0, :, kcols]], axis=0)
            v = jnp.concatenate([first_ref[0, :, vcols], second_ref[0, :, vcols]], axis=0)
            scores = (
                lax.dot_general(q, k, (((1,), (1,)), ((), ())), preferred_element_type=jnp.float32)
                * factor
            )
            top = jnp.max(scores, axis=-1, keepdims=True)
            expo = jnp.exp(scores - top)
            probs = expo / jnp.sum(expo, axis=-1, keepdims=True)
            probs_low = probs.astype(jnp.bfloat16)
            attended = jnp.dot(probs_low, v, preferred_element_type=jnp.float32)
            att_ref[rows, cols] = attended.astype(att_ref.dtype)
            grad_values = lax.dot_general(
                probs_low, g, (((0,), (0,)), ((), ())), preferred_element_type=jnp.float32
            )
            grad_probs = lax.dot_general(
                g, v, (((1,), (1,)), ((), ())), preferred_element_type=jnp.float32
            )
            grad_scores = probs * (
                grad_probs - jnp.sum(probs * grad_probs, axis=-1, keepdims=True)
            )
            grad_scores = grad_scores.astype(jnp.bfloat16)
            grad_keys = (
                lax.dot_general(
                    grad_scores, q, (((0,), (0,)), ((), ())), preferred_element_type=jnp.float32
                )
                * factor
            )
            acc_ref[first, :, kcols] += grad_keys[:NBR_LEN]
            acc_ref[second, :, kcols] += grad_keys[NBR_LEN:]
            acc_ref[first, :, vcols] += grad_values[:NBR_LEN]
            acc_ref[second, :, vcols] += grad_values[NBR_LEN:]

    @pl.when(step == pl.num_programs(0) - 1)
    def _():
        out_ref[...] = acc_ref[...].astype(out_ref.dtype)


def attention(owners, picks, queries, everyone, grad_attended, owner_count):
    rows, width = queries.shape
    per_step = 2
    steps = rows // (SPAN * per_step)
    heads = width // HD
    kv_width = everyone.shape[2]

    def neighbour_spec(index):
        return pl.BlockSpec(
            (1, NBR_LEN, kv_width), lambda c, o, n: (n[2 * per_step * c + index], 0, 0)
        )

    grid_spec = pltpu.PrefetchScalarGridSpec(
        num_scalar_prefetch=2,
        grid=(steps,),
        in_specs=[
            pl.BlockSpec((SPAN * per_step, width), lambda c, o, n: (c, 0)),
            pl.BlockSpec((SPAN * per_step, width), lambda c, o, n: (c, 0)),
        ]
        + [neighbour_spec(index) for index in range(2 * per_step)],
        out_specs=[
            pl.BlockSpec((SPAN * per_step, width), lambda c, o, n: (c, 0)),
            pl.BlockSpec((owner_count, NBR_LEN, kv_width), lambda c, o, n: (0, 0, 0)),
        ],
        scratch_shapes=[pltpu.VMEM((owner_count, NBR_LEN, kv_width), jnp.float32)],
    )
    return pl.pallas_call(
        functools.partial(attention_kernel, heads, per_step),
        grid_spec=grid_spec,
        out_shape=[
            jax.ShapeDtypeStruct((rows, width), jnp.bfloat16),
            jax.ShapeDtypeStruct((owner_count, NBR_LEN, kv_width), jnp.bfloat16),
        ],
        compiler_params=pltpu.CompilerParams(
            dimension_semantics=("arbitrary",), vmem_limit_bytes=56 * 1024 * 1024
        ),
    )(owners, picks, queries, grad_attended, *([everyone] * (2 * per_step)))


def slot_sum_kernel(readers, select_ref, returned_ref, out_ref):
    for slot in range(NB_DEV):
        total = returned_ref[0].astype(jnp.float32) * select_ref[0, slot]
        for r in range(1, readers):
            total = total + returned_ref[r].astype(jnp.float32) * select_ref[r, slot]
        out_ref[slot] = total.astype(out_ref.dtype)


def slot_sum(select, returned):
    readers, length, width = returned.shape
    tile = 768
    return pl.pallas_call(
        functools.partial(slot_sum_kernel, readers),
        grid=(width // tile,),
        in_specs=[
            pl.BlockSpec(memory_space=pltpu.SMEM),
            pl.BlockSpec((readers, length, tile), lambda j: (0, 0, j)),
        ],
        out_specs=pl.BlockSpec((NB_DEV, length, tile), lambda j: (0, 0, j)),
        out_shape=jax.ShapeDtypeStruct((NB_DEV, length, width), jnp.bfloat16),
    )(select, returned)


def local(kv_part, queries, w_out, d_out, nbr_owner, nbr_slot):
    dp_count = lax.axis_size("dp")
    reader = lax.axis_index("dp")
    head_width = w_out.shape[0]
    share_width = 2 * head_width
    span_count = queries.shape[0] // SPAN
    read_count = 2 * span_count
    shares = lax.psum_scatter(kv_part[0], "tensor", scatter_dimension=1, tiled=True)
    share_blocks = shares.reshape(NB_DEV, NBR_LEN, share_width)
    owner_ids = jnp.arange(dp_count, dtype=jnp.int32)
    slot_ids = jnp.arange(NB_DEV, dtype=jnp.int32)
    owner_hits = nbr_owner[:, :, None] == owner_ids[None, None, :]
    per_reader = owner_hits.reshape(dp_count, read_count, dp_count)
    reads_from = jnp.any(per_reader, axis=1)
    slot_from = jnp.max(jnp.where(per_reader, nbr_slot.reshape(dp_count, read_count, 1), 0), axis=1)
    my_owner = lax.dynamic_slice_in_dim(nbr_owner, reader * span_count, span_count, 0).reshape(
        read_count
    )
    my_slot = lax.dynamic_slice_in_dim(nbr_slot, reader * span_count, span_count, 0).reshape(
        read_count
    )
    serving = lax.dynamic_index_in_dim(reads_from, reader, 1, False)
    serving_slot = lax.dynamic_index_in_dim(slot_from, reader, 1, False)
    owner_select = ((serving_slot[:, None] == slot_ids[None, :]) & serving[:, None]).astype(
        jnp.float32
    )
    everyone = lax.all_gather(share_blocks, "dp", axis=0, tiled=True)
    picks = my_owner * NB_DEV + my_slot
    tensor_count = lax.axis_size("tensor")
    column = lax.axis_index("tensor")
    direction = 1 - 2 * (column % 2)
    ring = [(t, (t + 2 * (1 - 2 * (t % 2))) % tensor_count) for t in range(tensor_count)]
    swap = [(t, t ^ 1) for t in range(tensor_count)]
    hops = tensor_count // 2
    mine = [d_out]
    for _ in range(hops - 1):
        mine.append(lax.ppermute(mine[-1], "tensor", ring))
    theirs = [lax.ppermute(block, "tensor", swap) for block in mine]
    steps = jnp.arange(hops, dtype=jnp.int32)
    slot_block = jnp.concatenate(
        [
            (column - 2 * direction * steps) % tensor_count,
            ((column ^ 1) + 2 * direction * steps) % tensor_count,
        ]
    )
    block_slot = jnp.argmax(
        slot_block[None, :] == jnp.arange(tensor_count, dtype=jnp.int32)[:, None], axis=1
    )
    ordered = jnp.take(jnp.stack(mine + theirs), block_slot, axis=0, mode="clip")
    grad_attended = jnp.einsum(
        "tqc,htc->qh",
        ordered,
        w_out.reshape(head_width, tensor_count, d_out.shape[1]),
        preferred_element_type=jnp.float32,
    ).astype(jnp.bfloat16)
    attended, per_owner = attention(my_owner, picks, queries, everyone, grad_attended, dp_count)
    partial_out = jnp.dot(attended, w_out, preferred_element_type=jnp.float32)
    mixed = lax.psum_scatter(
        partial_out.astype(jnp.bfloat16), "tensor", scatter_dimension=1, tiled=True
    )
    returned = lax.all_to_all(per_owner, "dp", split_axis=0, concat_axis=0, tiled=True)
    owner_grad = slot_sum(owner_select, returned)
    d_kv = owner_grad.reshape(NB_DEV * NBR_LEN, share_width)
    return (mixed, d_kv)


def solution(mesh):
    placed = (
        P("tensor", "dp", None),
        P("dp", "tensor"),
        P("tensor", None),
        P("dp", "tensor"),
        P(),
        P(),
    )
    return jax.shard_map(
        local,
        mesh=mesh,
        in_specs=placed,
        out_specs=(P("dp", "tensor"), P("dp", "tensor")),
        check_vma=False,
    )
```

```python
import functools

import jax
import jax.numpy as jnp
from jax import lax
from jax.experimental import pallas as pl
from jax.experimental.pallas import tpu as pltpu
from jax.sharding import PartitionSpec as P

HD = 128
SPAN = 64
NBR_LEN = 128
NB_DEV = 2


def attention_kernel(heads, per_step, split, owner_ref, pick_ref, slot_ref, q_ref, g_ref, *rest):
    kv_refs = rest[: 2 * per_step]
    att_ref, spread_ref, out_ref, acc_ref = rest[2 * per_step:]
    factor = HD ** (-0.5)
    step = pl.program_id(0)

    @pl.when(step == 0)
    def _():
        acc_ref[...] = jnp.zeros_like(acc_ref)

    for sub in range(per_step):
        first_ref, second_ref = kv_refs[2 * sub], kv_refs[2 * sub + 1]
        span = step * per_step + sub
        first = owner_ref[2 * span]
        second = owner_ref[2 * span + 1]
        rows = slice(sub * SPAN, (sub + 1) * SPAN)
        for h in range(heads):
            cols = slice(h * HD, (h + 1) * HD)
            kcols = slice(2 * h * HD, 2 * h * HD + HD)
            vcols = slice(2 * h * HD + HD, 2 * (h + 1) * HD)
            q = q_ref[rows, cols]
            g = g_ref[rows, cols]
            k = jnp.concatenate([first_ref[0, :, kcols], second_ref[0, :, kcols]], axis=0)
            v = jnp.concatenate([first_ref[0, :, vcols], second_ref[0, :, vcols]], axis=0)
            scores = (
                lax.dot_general(q, k, (((1,), (1,)), ((), ())), preferred_element_type=jnp.float32)
                * factor
            )
            top = jnp.max(scores, axis=-1, keepdims=True)
            expo = jnp.exp(scores - top)
            probs = expo / jnp.sum(expo, axis=-1, keepdims=True)
            probs_low = probs.astype(jnp.bfloat16)
            attended = jnp.dot(probs_low, v, preferred_element_type=jnp.float32)
            att_ref[rows, cols] = attended.astype(att_ref.dtype)
            grad_values = lax.dot_general(
                probs_low, g, (((0,), (0,)), ((), ())), preferred_element_type=jnp.float32
            )
            grad_probs = lax.dot_general(
                g, v, (((1,), (1,)), ((), ())), preferred_element_type=jnp.float32
            )
            grad_scores = probs * (
                grad_probs - jnp.sum(probs * grad_probs, axis=-1, keepdims=True)
            )
            grad_scores = grad_scores.astype(jnp.bfloat16)
            grad_keys = (
                lax.dot_general(
                    grad_scores, q, (((0,), (0,)), ((), ())), preferred_element_type=jnp.float32
                )
                * factor
            )
            acc_ref[first, :, kcols] += grad_keys[:NBR_LEN]
            acc_ref[second, :, kcols] += grad_keys[NBR_LEN:]
            acc_ref[first, :, vcols] += grad_values[:NBR_LEN]
            acc_ref[second, :, vcols] += grad_values[NBR_LEN:]

    @pl.when(step == pl.num_programs(0) - 1)
    def _():
        out_ref[...] = acc_ref[:, :, split:].astype(out_ref.dtype)
        for owner in range(acc_ref.shape[0]):
            block = acc_ref[owner, :, :split]
            slot = slot_ref[owner]
            for target in range(NB_DEV):
                spread_ref[owner, target] = jnp.where(
                    slot == target, block, jnp.zeros_like(block)
                ).astype(spread_ref.dtype)


def attention(owners, picks, slots, queries, everyone, grad_attended, owner_count, split):
    rows, width = queries.shape
    per_step = 2
    steps = rows // (SPAN * per_step)
    heads = width // HD
    kv_width = everyone.shape[2]

    def neighbour_spec(index):
        return pl.BlockSpec(
            (1, NBR_LEN, kv_width), lambda c, o, n, s: (n[2 * per_step * c + index], 0, 0)
        )

    grid_spec = pltpu.PrefetchScalarGridSpec(
        num_scalar_prefetch=3,
        grid=(steps,),
        in_specs=[
            pl.BlockSpec((SPAN * per_step, width), lambda c, o, n, s: (c, 0)),
            pl.BlockSpec((SPAN * per_step, width), lambda c, o, n, s: (c, 0)),
        ]
        + [neighbour_spec(index) for index in range(2 * per_step)],
        out_specs=[
            pl.BlockSpec((SPAN * per_step, width), lambda c, o, n, s: (c, 0)),
            pl.BlockSpec((owner_count, NB_DEV, NBR_LEN, split), lambda c, o, n, s: (0, 0, 0, 0)),
            pl.BlockSpec((owner_count, NBR_LEN, kv_width - split), lambda c, o, n, s: (0, 0, 0)),
        ],
        scratch_shapes=[pltpu.VMEM((owner_count, NBR_LEN, kv_width), jnp.float32)],
    )
    return pl.pallas_call(
        functools.partial(attention_kernel, heads, per_step, split),
        grid_spec=grid_spec,
        out_shape=[
            jax.ShapeDtypeStruct((rows, width), jnp.bfloat16),
            jax.ShapeDtypeStruct((owner_count, NB_DEV, NBR_LEN, split), jnp.bfloat16),
            jax.ShapeDtypeStruct((owner_count, NBR_LEN, kv_width - split), jnp.bfloat16),
        ],
        compiler_params=pltpu.CompilerParams(
            dimension_semantics=("arbitrary",), vmem_limit_bytes=56 * 1024 * 1024
        ),
    )(owners, picks, slots, queries, grad_attended, *([everyone] * (2 * per_step)))


def slot_sum_kernel(readers, select_ref, returned_ref, out_ref):
    for slot in range(NB_DEV):
        total = returned_ref[0].astype(jnp.float32) * select_ref[0, slot]
        for r in range(1, readers):
            total = total + returned_ref[r].astype(jnp.float32) * select_ref[r, slot]
        out_ref[slot] = total.astype(out_ref.dtype)


def slot_sum(select, returned):
    readers, length, width = returned.shape
    tile = 384
    assert width % tile == 0
    return pl.pallas_call(
        functools.partial(slot_sum_kernel, readers),
        grid=(width // tile,),
        in_specs=[
            pl.BlockSpec(memory_space=pltpu.SMEM),
            pl.BlockSpec((readers, length, tile), lambda j: (0, 0, j)),
        ],
        out_specs=pl.BlockSpec((NB_DEV, length, tile), lambda j: (0, 0, j)),
        out_shape=jax.ShapeDtypeStruct((NB_DEV, length, width), jnp.bfloat16),
    )(select, returned)


def local(kv_part, queries, w_out, d_out, nbr_owner, nbr_slot):
    dp_count = lax.axis_size("dp")
    reader = lax.axis_index("dp")
    head_width = w_out.shape[0]
    share_width = 2 * head_width
    span_count = queries.shape[0] // SPAN
    read_count = 2 * span_count
    shares = lax.psum_scatter(kv_part[0], "tensor", scatter_dimension=1, tiled=True)
    share_blocks = shares.reshape(NB_DEV, NBR_LEN, share_width)
    owner_ids = jnp.arange(dp_count, dtype=jnp.int32)
    slot_ids = jnp.arange(NB_DEV, dtype=jnp.int32)
    owner_hits = nbr_owner[:, :, None] == owner_ids[None, None, :]
    per_reader = owner_hits.reshape(dp_count, read_count, dp_count)
    reads_from = jnp.any(per_reader, axis=1)
    slot_from = jnp.max(jnp.where(per_reader, nbr_slot.reshape(dp_count, read_count, 1), 0), axis=1)
    my_owner = lax.dynamic_slice_in_dim(nbr_owner, reader * span_count, span_count, 0).reshape(
        read_count
    )
    my_slot = lax.dynamic_slice_in_dim(nbr_slot, reader * span_count, span_count, 0).reshape(
        read_count
    )
    serving = lax.dynamic_index_in_dim(reads_from, reader, 1, False)
    serving_slot = lax.dynamic_index_in_dim(slot_from, reader, 1, False)
    owner_select = ((serving_slot[:, None] == slot_ids[None, :]) & serving[:, None]).astype(
        jnp.float32
    )
    everyone = lax.all_gather(share_blocks, "dp", axis=0, tiled=True)
    picks = my_owner * NB_DEV + my_slot
    tensor_count = lax.axis_size("tensor")
    column = lax.axis_index("tensor")
    direction = 1 - 2 * (column % 2)
    ring = [(t, (t + 2 * (1 - 2 * (t % 2))) % tensor_count) for t in range(tensor_count)]
    swap = [(t, t ^ 1) for t in range(tensor_count)]
    hops = tensor_count // 2
    mine = [d_out]
    for _ in range(hops - 1):
        mine.append(lax.ppermute(mine[-1], "tensor", ring))
    theirs = [lax.ppermute(block, "tensor", swap) for block in mine]
    steps = jnp.arange(hops, dtype=jnp.int32)
    slot_block = jnp.concatenate(
        [
            (column - 2 * direction * steps) % tensor_count,
            ((column ^ 1) + 2 * direction * steps) % tensor_count,
        ]
    )
    block_slot = jnp.argmax(
        slot_block[None, :] == jnp.arange(tensor_count, dtype=jnp.int32)[:, None], axis=1
    )
    ordered = jnp.take(jnp.stack(mine + theirs), block_slot, axis=0, mode="clip")
    grad_attended = jnp.einsum(
        "tqc,htc->qh",
        ordered,
        w_out.reshape(head_width, tensor_count, d_out.shape[1]),
        preferred_element_type=jnp.float32,
    ).astype(jnp.bfloat16)
    split = share_width // 4
    my_slots = lax.dynamic_index_in_dim(slot_from, reader, 0, False)
    attended, spread_part, per_owner = attention(
        my_owner, picks, my_slots, queries, everyone, grad_attended, dp_count, split
    )
    partial_out = jnp.dot(attended, w_out, preferred_element_type=jnp.float32)
    mixed = lax.psum_scatter(
        partial_out.astype(jnp.bfloat16), "tensor", scatter_dimension=1, tiled=True
    )
    reduced_part = lax.psum_scatter(
        spread_part.reshape(dp_count * NB_DEV, NBR_LEN, split), "dp", scatter_dimension=0, tiled=True
    )
    returned = lax.all_to_all(per_owner, "dp", split_axis=0, concat_axis=0, tiled=True)
    owner_grad = jnp.concatenate([reduced_part, slot_sum(owner_select, returned)], axis=2)
    d_kv = owner_grad.reshape(NB_DEV * NBR_LEN, share_width)
    return (mixed, d_kv)


def solution(mesh):
    placed = (
        P("tensor", "dp", None),
        P("dp", "tensor"),
        P("tensor", None),
        P("dp", "tensor"),
        P(),
        P(),
    )
    return jax.shard_map(
        local,
        mesh=mesh,
        in_specs=placed,
        out_specs=(P("dp", "tensor"), P("dp", "tensor")),
        check_vma=False,
    )
```

```python
import functools

import jax
import jax.numpy as jnp
from jax import lax
from jax.experimental import pallas as pl
from jax.experimental.pallas import tpu as pltpu
from jax.sharding import PartitionSpec as P

HD = 128
SPAN = 64
NBR_LEN = 128
NB_DEV = 2


def attention_kernel(heads, per_step, owner_ref, pick_ref, q_ref, g_ref, *rest):
    kv_refs = rest[: 2 * per_step]
    att_ref, out_ref, acc_ref = rest[2 * per_step:]
    factor = HD ** (-0.5)
    step = pl.program_id(0)

    @pl.when(step == 0)
    def _():
        acc_ref[...] = jnp.zeros_like(acc_ref)

    for sub in range(per_step):
        first_ref, second_ref = kv_refs[2 * sub], kv_refs[2 * sub + 1]
        span = step * per_step + sub
        first = owner_ref[2 * span]
        second = owner_ref[2 * span + 1]
        rows = slice(sub * SPAN, (sub + 1) * SPAN)
        head_cols = [slice(h * HD, (h + 1) * HD) for h in range(heads)]
        key_cols = [slice(2 * h * HD, 2 * h * HD + HD) for h in range(heads)]
        value_cols = [slice(2 * h * HD + HD, 2 * (h + 1) * HD) for h in range(heads)]
        q = jnp.stack([q_ref[rows, c] for c in head_cols])
        g = jnp.stack([g_ref[rows, c] for c in head_cols])
        k = jnp.stack(
            [jnp.concatenate([first_ref[0, :, c], second_ref[0, :, c]], axis=0) for c in key_cols]
        )
        v = jnp.stack(
            [jnp.concatenate([first_ref[0, :, c], second_ref[0, :, c]], axis=0) for c in value_cols]
        )
        batch_nt = (((2,), (2,)), ((0,), (0,)))
        batch_nn = (((2,), (1,)), ((0,), (0,)))
        batch_tn = (((1,), (1,)), ((0,), (0,)))
        scores = lax.dot_general(q, k, batch_nt, preferred_element_type=jnp.float32) * factor
        top = jnp.max(scores, axis=-1, keepdims=True)
        expo = jnp.exp(scores - top)
        probs = expo / jnp.sum(expo, axis=-1, keepdims=True)
        probs_low = probs.astype(jnp.bfloat16)
        attended = lax.dot_general(probs_low, v, batch_nn, preferred_element_type=jnp.float32)
        grad_values = lax.dot_general(probs_low, g, batch_tn, preferred_element_type=jnp.float32)
        grad_probs = lax.dot_general(g, v, batch_nt, preferred_element_type=jnp.float32)
        grad_scores = probs * (grad_probs - jnp.sum(probs * grad_probs, axis=-1, keepdims=True))
        grad_scores = grad_scores.astype(jnp.bfloat16)
        grad_keys = (
            lax.dot_general(grad_scores, q, batch_tn, preferred_element_type=jnp.float32) * factor
        )
        for h in range(heads):
            att_ref[rows, head_cols[h]] = attended[h].astype(att_ref.dtype)
            acc_ref[first, :, key_cols[h]] += grad_keys[h, :NBR_LEN]
            acc_ref[second, :, key_cols[h]] += grad_keys[h, NBR_LEN:]
            acc_ref[first, :, value_cols[h]] += grad_values[h, :NBR_LEN]
            acc_ref[second, :, value_cols[h]] += grad_values[h, NBR_LEN:]

    @pl.when(step == pl.num_programs(0) - 1)
    def _():
        out_ref[...] = acc_ref[...].astype(out_ref.dtype)


def attention(owners, picks, queries, everyone, grad_attended, owner_count):
    rows, width = queries.shape
    per_step = 2
    steps = rows // (SPAN * per_step)
    heads = width // HD
    kv_width = everyone.shape[2]

    def neighbour_spec(index):
        return pl.BlockSpec(
            (1, NBR_LEN, kv_width), lambda c, o, n: (n[2 * per_step * c + index], 0, 0)
        )

    grid_spec = pltpu.PrefetchScalarGridSpec(
        num_scalar_prefetch=2,
        grid=(steps,),
        in_specs=[
            pl.BlockSpec((SPAN * per_step, width), lambda c, o, n: (c, 0)),
            pl.BlockSpec((SPAN * per_step, width), lambda c, o, n: (c, 0)),
        ]
        + [neighbour_spec(index) for index in range(2 * per_step)],
        out_specs=[
            pl.BlockSpec((SPAN * per_step, width), lambda c, o, n: (c, 0)),
            pl.BlockSpec((owner_count, NBR_LEN, kv_width), lambda c, o, n: (0, 0, 0)),
        ],
        scratch_shapes=[pltpu.VMEM((owner_count, NBR_LEN, kv_width), jnp.float32)],
    )
    return pl.pallas_call(
        functools.partial(attention_kernel, heads, per_step),
        grid_spec=grid_spec,
        out_shape=[
            jax.ShapeDtypeStruct((rows, width), jnp.bfloat16),
            jax.ShapeDtypeStruct((owner_count, NBR_LEN, kv_width), jnp.bfloat16),
        ],
        compiler_params=pltpu.CompilerParams(
            dimension_semantics=("arbitrary",), vmem_limit_bytes=56 * 1024 * 1024
        ),
    )(owners, picks, queries, grad_attended, *([everyone] * (2 * per_step)))


def slot_sum_kernel(readers, select_ref, returned_ref, out_ref):
    for slot in range(NB_DEV):
        total = returned_ref[0].astype(jnp.float32) * select_ref[0, slot]
        for r in range(1, readers):
            total = total + returned_ref[r].astype(jnp.float32) * select_ref[r, slot]
        out_ref[slot] = total.astype(out_ref.dtype)


def slot_sum(select, returned):
    readers, length, width = returned.shape
    tile = 768
    return pl.pallas_call(
        functools.partial(slot_sum_kernel, readers),
        grid=(width // tile,),
        in_specs=[
            pl.BlockSpec(memory_space=pltpu.SMEM),
            pl.BlockSpec((readers, length, tile), lambda j: (0, 0, j)),
        ],
        out_specs=pl.BlockSpec((NB_DEV, length, tile), lambda j: (0, 0, j)),
        out_shape=jax.ShapeDtypeStruct((NB_DEV, length, width), jnp.bfloat16),
    )(select, returned)


def local(kv_part, queries, w_out, d_out, nbr_owner, nbr_slot):
    dp_count = lax.axis_size("dp")
    reader = lax.axis_index("dp")
    head_width = w_out.shape[0]
    share_width = 2 * head_width
    span_count = queries.shape[0] // SPAN
    read_count = 2 * span_count
    shares = lax.psum_scatter(kv_part[0], "tensor", scatter_dimension=1, tiled=True)
    share_blocks = shares.reshape(NB_DEV, NBR_LEN, share_width)
    owner_ids = jnp.arange(dp_count, dtype=jnp.int32)
    slot_ids = jnp.arange(NB_DEV, dtype=jnp.int32)
    owner_hits = nbr_owner[:, :, None] == owner_ids[None, None, :]
    per_reader = owner_hits.reshape(dp_count, read_count, dp_count)
    reads_from = jnp.any(per_reader, axis=1)
    slot_from = jnp.max(jnp.where(per_reader, nbr_slot.reshape(dp_count, read_count, 1), 0), axis=1)
    my_owner = lax.dynamic_slice_in_dim(nbr_owner, reader * span_count, span_count, 0).reshape(
        read_count
    )
    my_slot = lax.dynamic_slice_in_dim(nbr_slot, reader * span_count, span_count, 0).reshape(
        read_count
    )
    serving = lax.dynamic_index_in_dim(reads_from, reader, 1, False)
    serving_slot = lax.dynamic_index_in_dim(slot_from, reader, 1, False)
    owner_select = ((serving_slot[:, None] == slot_ids[None, :]) & serving[:, None]).astype(
        jnp.float32
    )
    everyone = lax.all_gather(share_blocks, "dp", axis=0, tiled=True)
    picks = my_owner * NB_DEV + my_slot
    tensor_count = lax.axis_size("tensor")
    column = lax.axis_index("tensor")
    direction = 1 - 2 * (column % 2)
    ring = [(t, (t + 2 * (1 - 2 * (t % 2))) % tensor_count) for t in range(tensor_count)]
    swap = [(t, t ^ 1) for t in range(tensor_count)]
    hops = tensor_count // 2
    mine = [d_out]
    for _ in range(hops - 1):
        mine.append(lax.ppermute(mine[-1], "tensor", ring))
    theirs = [lax.ppermute(block, "tensor", swap) for block in mine]
    steps = jnp.arange(hops, dtype=jnp.int32)
    slot_block = jnp.concatenate(
        [
            (column - 2 * direction * steps) % tensor_count,
            ((column ^ 1) + 2 * direction * steps) % tensor_count,
        ]
    )
    block_slot = jnp.argmax(
        slot_block[None, :] == jnp.arange(tensor_count, dtype=jnp.int32)[:, None], axis=1
    )
    ordered = jnp.take(jnp.stack(mine + theirs), block_slot, axis=0, mode="clip")
    grad_attended = jnp.einsum(
        "tqc,htc->qh",
        ordered,
        w_out.reshape(head_width, tensor_count, d_out.shape[1]),
        preferred_element_type=jnp.float32,
    ).astype(jnp.bfloat16)
    attended, per_owner = attention(my_owner, picks, queries, everyone, grad_attended, dp_count)
    partial_out = jnp.dot(attended, w_out, preferred_element_type=jnp.float32)
    mixed = lax.psum_scatter(
        partial_out.astype(jnp.bfloat16), "tensor", scatter_dimension=1, tiled=True
    )
    returned = lax.all_to_all(per_owner, "dp", split_axis=0, concat_axis=0, tiled=True)
    owner_grad = slot_sum(owner_select, returned)
    d_kv = owner_grad.reshape(NB_DEV * NBR_LEN, share_width)
    return (mixed, d_kv)


def solution(mesh):
    placed = (
        P("tensor", "dp", None),
        P("dp", "tensor"),
        P("tensor", None),
        P("dp", "tensor"),
        P(),
        P(),
    )
    return jax.shard_map(
        local,
        mesh=mesh,
        in_specs=placed,
        out_specs=(P("dp", "tensor"), P("dp", "tensor")),
        check_vma=False,
    )
```

```python
import functools

import jax
import jax.numpy as jnp
from jax import lax
from jax.experimental import pallas as pl
from jax.experimental.pallas import tpu as pltpu
from jax.sharding import PartitionSpec as P

HD = 128
SPAN = 64
NBR_LEN = 128
NB_DEV = 2


def attention_kernel(heads, per_step, owner_ref, pick_ref, q_ref, g_ref, *rest):
    kv_refs = rest[: 2 * per_step]
    att_ref, out_ref, acc_ref = rest[2 * per_step:]
    factor = HD ** (-0.5)
    step = pl.program_id(0)

    @pl.when(step == 0)
    def _():
        acc_ref[...] = jnp.zeros_like(acc_ref)

    for sub in range(per_step):
        first_ref, second_ref = kv_refs[2 * sub], kv_refs[2 * sub + 1]
        span = step * per_step + sub
        first = owner_ref[2 * span]
        second = owner_ref[2 * span + 1]
        rows = slice(sub * SPAN, (sub + 1) * SPAN)
        head_cols = [slice(h * HD, (h + 1) * HD) for h in range(heads)]
        key_cols = [slice(2 * h * HD, 2 * h * HD + HD) for h in range(heads)]
        value_cols = [slice(2 * h * HD + HD, 2 * (h + 1) * HD) for h in range(heads)]
        q = jnp.stack([q_ref[rows, c] for c in head_cols])
        g = jnp.stack([g_ref[rows, c] for c in head_cols])
        k = jnp.stack(
            [jnp.concatenate([first_ref[0, :, c], second_ref[0, :, c]], axis=0) for c in key_cols]
        )
        v = jnp.stack(
            [jnp.concatenate([first_ref[0, :, c], second_ref[0, :, c]], axis=0) for c in value_cols]
        )
        batch_nt = (((2,), (2,)), ((0,), (0,)))
        batch_nn = (((2,), (1,)), ((0,), (0,)))
        batch_tn = (((1,), (1,)), ((0,), (0,)))
        scores = lax.dot_general(q, k, batch_nt, preferred_element_type=jnp.float32) * factor
        top = jnp.max(scores, axis=-1, keepdims=True)
        expo = jnp.exp(scores - top)
        probs = expo / jnp.sum(expo, axis=-1, keepdims=True)
        probs_low = probs.astype(jnp.bfloat16)
        attended = lax.dot_general(probs_low, v, batch_nn, preferred_element_type=jnp.float32)
        grad_values = lax.dot_general(probs_low, g, batch_tn, preferred_element_type=jnp.float32)
        grad_probs = lax.dot_general(g, v, batch_nt, preferred_element_type=jnp.float32)
        grad_scores = probs * (grad_probs - jnp.sum(probs * grad_probs, axis=-1, keepdims=True))
        grad_scores = grad_scores.astype(jnp.bfloat16)
        grad_keys = (
            lax.dot_general(grad_scores, q, batch_tn, preferred_element_type=jnp.float32) * factor
        )
        for h in range(heads):
            att_ref[rows, head_cols[h]] = attended[h].astype(att_ref.dtype)
            acc_ref[first, :, key_cols[h]] += grad_keys[h, :NBR_LEN]
            acc_ref[second, :, key_cols[h]] += grad_keys[h, NBR_LEN:]
            acc_ref[first, :, value_cols[h]] += grad_values[h, :NBR_LEN]
            acc_ref[second, :, value_cols[h]] += grad_values[h, NBR_LEN:]

    @pl.when(step == pl.num_programs(0) - 1)
    def _():
        out_ref[...] = acc_ref[...].astype(out_ref.dtype)


def attention(owners, picks, queries, everyone, grad_attended, owner_count):
    rows, width = queries.shape
    per_step = 2
    steps = rows // (SPAN * per_step)
    heads = width // HD
    kv_width = everyone.shape[2]

    def neighbour_spec(index):
        return pl.BlockSpec(
            (1, NBR_LEN, kv_width), lambda c, o, n: (n[2 * per_step * c + index], 0, 0)
        )

    grid_spec = pltpu.PrefetchScalarGridSpec(
        num_scalar_prefetch=2,
        grid=(steps,),
        in_specs=[
            pl.BlockSpec((SPAN * per_step, width), lambda c, o, n: (c, 0)),
            pl.BlockSpec((SPAN * per_step, width), lambda c, o, n: (c, 0)),
        ]
        + [neighbour_spec(index) for index in range(2 * per_step)],
        out_specs=[
            pl.BlockSpec((SPAN * per_step, width), lambda c, o, n: (c, 0)),
            pl.BlockSpec((owner_count, NBR_LEN, kv_width), lambda c, o, n: (0, 0, 0)),
        ],
        scratch_shapes=[pltpu.VMEM((owner_count, NBR_LEN, kv_width), jnp.float32)],
    )
    return pl.pallas_call(
        functools.partial(attention_kernel, heads, per_step),
        grid_spec=grid_spec,
        out_shape=[
            jax.ShapeDtypeStruct((rows, width), jnp.bfloat16),
            jax.ShapeDtypeStruct((owner_count, NBR_LEN, kv_width), jnp.bfloat16),
        ],
        compiler_params=pltpu.CompilerParams(
            dimension_semantics=("arbitrary",), vmem_limit_bytes=56 * 1024 * 1024
        ),
    )(owners, picks, queries, grad_attended, *([everyone] * (2 * per_step)))


def slot_sum_kernel(readers, select_ref, returned_ref, out_ref):
    for slot in range(NB_DEV):
        total = returned_ref[0].astype(jnp.float32) * select_ref[0, slot]
        for r in range(1, readers):
            total = total + returned_ref[r].astype(jnp.float32) * select_ref[r, slot]
        out_ref[slot] = total.astype(out_ref.dtype)


def slot_sum(select, returned):
    readers, length, width = returned.shape
    tile = 768
    return pl.pallas_call(
        functools.partial(slot_sum_kernel, readers),
        grid=(width // tile,),
        in_specs=[
            pl.BlockSpec(memory_space=pltpu.SMEM),
            pl.BlockSpec((readers, length, tile), lambda j: (0, 0, j)),
        ],
        out_specs=pl.BlockSpec((NB_DEV, length, tile), lambda j: (0, 0, j)),
        out_shape=jax.ShapeDtypeStruct((NB_DEV, length, width), jnp.bfloat16),
    )(select, returned)


def local(kv_part, queries, w_out, d_out, nbr_owner, nbr_slot):
    dp_count = lax.axis_size("dp")
    reader = lax.axis_index("dp")
    head_width = w_out.shape[0]
    share_width = 2 * head_width
    span_count = queries.shape[0] // SPAN
    read_count = 2 * span_count
    by_column = kv_part[0].reshape(NB_DEV * NBR_LEN, -1, share_width).transpose(1, 0, 2)
    shares = lax.psum_scatter(by_column, "tensor", scatter_dimension=0, tiled=True)
    share_blocks = shares.reshape(NB_DEV, NBR_LEN, share_width)
    owner_ids = jnp.arange(dp_count, dtype=jnp.int32)
    slot_ids = jnp.arange(NB_DEV, dtype=jnp.int32)
    owner_hits = nbr_owner[:, :, None] == owner_ids[None, None, :]
    per_reader = owner_hits.reshape(dp_count, read_count, dp_count)
    reads_from = jnp.any(per_reader, axis=1)
    slot_from = jnp.max(jnp.where(per_reader, nbr_slot.reshape(dp_count, read_count, 1), 0), axis=1)
    my_owner = lax.dynamic_slice_in_dim(nbr_owner, reader * span_count, span_count, 0).reshape(
        read_count
    )
    my_slot = lax.dynamic_slice_in_dim(nbr_slot, reader * span_count, span_count, 0).reshape(
        read_count
    )
    serving = lax.dynamic_index_in_dim(reads_from, reader, 1, False)
    serving_slot = lax.dynamic_index_in_dim(slot_from, reader, 1, False)
    owner_select = ((serving_slot[:, None] == slot_ids[None, :]) & serving[:, None]).astype(
        jnp.float32
    )
    everyone = lax.all_gather(share_blocks, "dp", axis=0, tiled=True)
    picks = my_owner * NB_DEV + my_slot
    tensor_count = lax.axis_size("tensor")
    column = lax.axis_index("tensor")
    direction = 1 - 2 * (column % 2)
    ring = [(t, (t + 2 * (1 - 2 * (t % 2))) % tensor_count) for t in range(tensor_count)]
    swap = [(t, t ^ 1) for t in range(tensor_count)]
    hops = tensor_count // 2
    mine = [d_out]
    for _ in range(hops - 1):
        mine.append(lax.ppermute(mine[-1], "tensor", ring))
    theirs = [lax.ppermute(block, "tensor", swap) for block in mine]
    steps = jnp.arange(hops, dtype=jnp.int32)
    slot_block = jnp.concatenate(
        [
            (column - 2 * direction * steps) % tensor_count,
            ((column ^ 1) + 2 * direction * steps) % tensor_count,
        ]
    )
    block_slot = jnp.argmax(
        slot_block[None, :] == jnp.arange(tensor_count, dtype=jnp.int32)[:, None], axis=1
    )
    ordered = jnp.take(jnp.stack(mine + theirs), block_slot, axis=0, mode="clip")
    grad_attended = jnp.einsum(
        "tqc,htc->qh",
        ordered,
        w_out.reshape(head_width, tensor_count, d_out.shape[1]),
        preferred_element_type=jnp.float32,
    ).astype(jnp.bfloat16)
    attended, per_owner = attention(my_owner, picks, queries, everyone, grad_attended, dp_count)
    partial_out = jnp.dot(attended, w_out, preferred_element_type=jnp.float32)
    mixed = lax.psum_scatter(
        partial_out.astype(jnp.bfloat16), "tensor", scatter_dimension=1, tiled=True
    )
    returned = lax.all_to_all(per_owner, "dp", split_axis=0, concat_axis=0, tiled=True)
    owner_grad = slot_sum(owner_select, returned)
    d_kv = owner_grad.reshape(NB_DEV * NBR_LEN, share_width)
    return (mixed, d_kv)


def solution(mesh):
    placed = (
        P("tensor", "dp", None),
        P("dp", "tensor"),
        P("tensor", None),
        P("dp", "tensor"),
        P(),
        P(),
    )
    return jax.shard_map(
        local,
        mesh=mesh,
        in_specs=placed,
        out_specs=(P("dp", "tensor"), P("dp", "tensor")),
        check_vma=False,
    )
```

```python
import functools

import jax
import jax.numpy as jnp
from jax import lax
from jax.experimental import pallas as pl
from jax.experimental.pallas import tpu as pltpu
from jax.sharding import PartitionSpec as P

HD = 128
SPAN = 64
NBR_LEN = 128
NB_DEV = 2


def attention_kernel(heads, per_step, owner_ref, pick_ref, q_ref, g_ref, *rest):
    kv_refs = rest[: 2 * per_step]
    att_ref, out_ref, acc_ref = rest[2 * per_step:]
    factor = HD ** (-0.5)
    step = pl.program_id(0)

    @pl.when(step == 0)
    def _():
        acc_ref[...] = jnp.zeros_like(acc_ref)

    for sub in range(per_step):
        first_ref, second_ref = kv_refs[2 * sub], kv_refs[2 * sub + 1]
        span = step * per_step + sub
        first = owner_ref[2 * span]
        second = owner_ref[2 * span + 1]
        rows = slice(sub * SPAN, (sub + 1) * SPAN)
        head_cols = [slice(h * HD, (h + 1) * HD) for h in range(heads)]
        key_cols = [slice(2 * h * HD, 2 * h * HD + HD) for h in range(heads)]
        value_cols = [slice(2 * h * HD + HD, 2 * (h + 1) * HD) for h in range(heads)]
        q = jnp.stack([q_ref[rows, c] for c in head_cols])
        g = jnp.stack([g_ref[rows, c] for c in head_cols])
        k = jnp.stack(
            [jnp.concatenate([first_ref[0, :, c], second_ref[0, :, c]], axis=0) for c in key_cols]
        )
        v = jnp.stack(
            [jnp.concatenate([first_ref[0, :, c], second_ref[0, :, c]], axis=0) for c in value_cols]
        )
        batch_nt = (((2,), (2,)), ((0,), (0,)))
        batch_nn = (((2,), (1,)), ((0,), (0,)))
        batch_tn = (((1,), (1,)), ((0,), (0,)))
        scores = lax.dot_general(q, k, batch_nt, preferred_element_type=jnp.float32) * factor
        top = jnp.max(scores, axis=-1, keepdims=True)
        expo = jnp.exp(scores - top)
        probs = expo / jnp.sum(expo, axis=-1, keepdims=True)
        probs_low = probs.astype(jnp.bfloat16)
        attended = lax.dot_general(probs_low, v, batch_nn, preferred_element_type=jnp.float32)
        grad_values = lax.dot_general(probs_low, g, batch_tn, preferred_element_type=jnp.float32)
        grad_probs = lax.dot_general(g, v, batch_nt, preferred_element_type=jnp.float32)
        grad_scores = probs * (grad_probs - jnp.sum(probs * grad_probs, axis=-1, keepdims=True))
        grad_scores = grad_scores.astype(jnp.bfloat16)
        grad_keys = (
            lax.dot_general(grad_scores, q, batch_tn, preferred_element_type=jnp.float32) * factor
        )
        for h in range(heads):
            att_ref[rows, head_cols[h]] = attended[h].astype(att_ref.dtype)
        for owner, part in ((first, slice(0, NBR_LEN)), (second, slice(NBR_LEN, 2 * NBR_LEN))):
            pieces = []
            for h in range(heads):
                pieces += [grad_keys[h, part], grad_values[h, part]]
            acc_ref[owner] += jnp.concatenate(pieces, axis=1)

    @pl.when(step == pl.num_programs(0) - 1)
    def _():
        out_ref[...] = acc_ref[...].astype(out_ref.dtype)


def attention(owners, picks, queries, everyone, grad_attended, owner_count):
    rows, width = queries.shape
    per_step = 2
    steps = rows // (SPAN * per_step)
    heads = width // HD
    kv_width = everyone.shape[2]

    def neighbour_spec(index):
        return pl.BlockSpec(
            (1, NBR_LEN, kv_width), lambda c, o, n: (n[2 * per_step * c + index], 0, 0)
        )

    grid_spec = pltpu.PrefetchScalarGridSpec(
        num_scalar_prefetch=2,
        grid=(steps,),
        in_specs=[
            pl.BlockSpec((SPAN * per_step, width), lambda c, o, n: (c, 0)),
            pl.BlockSpec((SPAN * per_step, width), lambda c, o, n: (c, 0)),
        ]
        + [neighbour_spec(index) for index in range(2 * per_step)],
        out_specs=[
            pl.BlockSpec((SPAN * per_step, width), lambda c, o, n: (c, 0)),
            pl.BlockSpec((owner_count, NBR_LEN, kv_width), lambda c, o, n: (0, 0, 0)),
        ],
        scratch_shapes=[pltpu.VMEM((owner_count, NBR_LEN, kv_width), jnp.float32)],
    )
    return pl.pallas_call(
        functools.partial(attention_kernel, heads, per_step),
        grid_spec=grid_spec,
        out_shape=[
            jax.ShapeDtypeStruct((rows, width), jnp.bfloat16),
            jax.ShapeDtypeStruct((owner_count, NBR_LEN, kv_width), jnp.bfloat16),
        ],
        compiler_params=pltpu.CompilerParams(
            dimension_semantics=("arbitrary",), vmem_limit_bytes=56 * 1024 * 1024
        ),
    )(owners, picks, queries, grad_attended, *([everyone] * (2 * per_step)))


def slot_sum_kernel(readers, select_ref, returned_ref, out_ref):
    for slot in range(NB_DEV):
        total = returned_ref[0].astype(jnp.float32) * select_ref[0, slot]
        for r in range(1, readers):
            total = total + returned_ref[r].astype(jnp.float32) * select_ref[r, slot]
        out_ref[slot] = total.astype(out_ref.dtype)


def slot_sum(select, returned):
    readers, length, width = returned.shape
    tile = 768
    return pl.pallas_call(
        functools.partial(slot_sum_kernel, readers),
        grid=(width // tile,),
        in_specs=[
            pl.BlockSpec(memory_space=pltpu.SMEM),
            pl.BlockSpec((readers, length, tile), lambda j: (0, 0, j)),
        ],
        out_specs=pl.BlockSpec((NB_DEV, length, tile), lambda j: (0, 0, j)),
        out_shape=jax.ShapeDtypeStruct((NB_DEV, length, width), jnp.bfloat16),
    )(select, returned)


def local(kv_part, queries, w_out, d_out, nbr_owner, nbr_slot):
    dp_count = lax.axis_size("dp")
    reader = lax.axis_index("dp")
    head_width = w_out.shape[0]
    share_width = 2 * head_width
    span_count = queries.shape[0] // SPAN
    read_count = 2 * span_count
    shares = lax.psum_scatter(kv_part[0], "tensor", scatter_dimension=1, tiled=True)
    share_blocks = shares.reshape(NB_DEV, NBR_LEN, share_width)
    owner_ids = jnp.arange(dp_count, dtype=jnp.int32)
    slot_ids = jnp.arange(NB_DEV, dtype=jnp.int32)
    owner_hits = nbr_owner[:, :, None] == owner_ids[None, None, :]
    per_reader = owner_hits.reshape(dp_count, read_count, dp_count)
    reads_from = jnp.any(per_reader, axis=1)
    slot_from = jnp.max(jnp.where(per_reader, nbr_slot.reshape(dp_count, read_count, 1), 0), axis=1)
    my_owner = lax.dynamic_slice_in_dim(nbr_owner, reader * span_count, span_count, 0).reshape(
        read_count
    )
    my_slot = lax.dynamic_slice_in_dim(nbr_slot, reader * span_count, span_count, 0).reshape(
        read_count
    )
    serving = lax.dynamic_index_in_dim(reads_from, reader, 1, False)
    serving_slot = lax.dynamic_index_in_dim(slot_from, reader, 1, False)
    owner_select = ((serving_slot[:, None] == slot_ids[None, :]) & serving[:, None]).astype(
        jnp.float32
    )
    everyone = lax.all_gather(share_blocks, "dp", axis=0, tiled=True)
    picks = my_owner * NB_DEV + my_slot
    tensor_count = lax.axis_size("tensor")
    column = lax.axis_index("tensor")
    direction = 1 - 2 * (column % 2)
    ring = [(t, (t + 2 * (1 - 2 * (t % 2))) % tensor_count) for t in range(tensor_count)]
    swap = [(t, t ^ 1) for t in range(tensor_count)]
    hops = tensor_count // 2
    mine = [d_out]
    for _ in range(hops - 1):
        mine.append(lax.ppermute(mine[-1], "tensor", ring))
    theirs = [lax.ppermute(block, "tensor", swap) for block in mine]
    steps = jnp.arange(hops, dtype=jnp.int32)
    slot_block = jnp.concatenate(
        [
            (column - 2 * direction * steps) % tensor_count,
            ((column ^ 1) + 2 * direction * steps) % tensor_count,
        ]
    )
    block_slot = jnp.argmax(
        slot_block[None, :] == jnp.arange(tensor_count, dtype=jnp.int32)[:, None], axis=1
    )
    ordered = jnp.take(jnp.stack(mine + theirs), block_slot, axis=0, mode="clip")
    grad_attended = jnp.einsum(
        "tqc,htc->qh",
        ordered,
        w_out.reshape(head_width, tensor_count, d_out.shape[1]),
        preferred_element_type=jnp.float32,
    ).astype(jnp.bfloat16)
    attended, per_owner = attention(my_owner, picks, queries, everyone, grad_attended, dp_count)
    partial_out = jnp.dot(attended, w_out, preferred_element_type=jnp.float32)
    mixed = lax.psum_scatter(
        partial_out.astype(jnp.bfloat16), "tensor", scatter_dimension=1, tiled=True
    )
    returned = lax.all_to_all(per_owner, "dp", split_axis=0, concat_axis=0, tiled=True)
    owner_grad = slot_sum(owner_select, returned)
    d_kv = owner_grad.reshape(NB_DEV * NBR_LEN, share_width)
    return (mixed, d_kv)


def solution(mesh):
    placed = (
        P("tensor", "dp", None),
        P("dp", "tensor"),
        P("tensor", None),
        P("dp", "tensor"),
        P(),
        P(),
    )
    return jax.shard_map(
        local,
        mesh=mesh,
        in_specs=placed,
        out_specs=(P("dp", "tensor"), P("dp", "tensor")),
        check_vma=False,
    )
```
